256 devices in a mesh: rows: 32 (over y_lo, z, core), protos: 8 (over y_hi, x).
Axes of the slice: x: 4, y: 4 (y_hi: 2, y_lo: 2; y = y_hi * 2 + y_lo), z: 8, core: 2. Of those that a mesh axis runs over, the one named last changes fastest.
Arguments:
- teacher: bfloat16 [2048, 256], P('rows')
- students: bfloat16 [8192, 256], P('rows')
- prototypes: bfloat16 [256, 65536], P(None, 'protos')
- pairing: int32 [8192], P('rows'), may hold values from 0 to 63
- layout: int32 [8192], P('rows'), may hold values from 0 to 31, as said below
Outputs:
- grad_students: float32 [8192, 256], P('rows')
- grad_protos: float32 [256, 65536], P('rows', 'protos')
The draws below stay inside these ranges and needn't reach their ends.
Inputs may be any that keep to these rules, and one draw needn't show every extreme that they name: `layout`: in each aligned block of 256 rows, every value appears exactly 8 times.
All inputs are finite; a program needn't handle non-finite values.
Results may differ from the reference program's by a relative error of at most 0.0003.
The reference program's roundings to bfloat16 on the way (of `w_unit_b`, `tea_unit_b`, `stu_unit_b` and `grad_logits`) count: a program that leaves them out, or rounds other values in their place, can miss the bound.
Values may be sent and summed in bfloat16 or wider, within the bound.
A program may use at most 64 MiB of HBM per device.

```python
import math
import jax
import jax.numpy as jnp
from jax import lax

D = 256
PROTOS = 65536
TEA_DEV = 64
ITERS = 2
TEACHERS = 2048
STU_DEV = 256
STUDENTS = 8192
BUCKET = 8


cluster_count = 4


def cluster_centers(key):
    raw_centers = jax.random.normal(jax.random.fold_in(key, 101), (cluster_count, D), jnp.float32)
    return raw_centers / jnp.sqrt(jnp.sum(raw_centers * raw_centers, 1, keepdims=True))


def clustered(key, salt, amount):
    cluster_ids = jax.random.randint(jax.random.fold_in(key, salt), (amount,), 0, cluster_count)
    jitter = jax.random.normal(jax.random.fold_in(key, salt + 1), (amount, D), jnp.float32) / math.sqrt(D)
    vectors = 0.85 * cluster_centers(key)[cluster_ids] + 0.5 * jitter
    return vectors


def draw_teacher(key, part):
    return clustered(key, 1, TEACHERS).astype(jnp.bfloat16)


def draw_students(key, part):
    return clustered(key, 11, STUDENTS).astype(jnp.bfloat16)


def draw_prototypes(key, part):
    return clustered(key, 21, PROTOS).T.astype(jnp.bfloat16)


def draw_layout(key, part):
    block_count = STUDENTS // STU_DEV
    groups = STU_DEV // BUCKET
    labels = jnp.repeat(jnp.arange(groups, dtype=jnp.int32), BUCKET)
    block_keys = jax.random.split(jax.random.fold_in(key, 31), block_count)
    mixed = jax.vmap(lambda one_key: jax.random.permutation(one_key, labels))(block_keys)
    return mixed.reshape(-1).astype(jnp.int32)


def place_ends(result, key, smallest, high):
    index_at = [jax.random.randint(jax.random.fold_in(key, axis), (), 0, length) for axis, length in enumerate(result.shape)]
    longest = result.shape.index(max(result.shape))
    beside = index_at[:longest] + [(index_at[longest] + 1) % result.shape[longest]] + index_at[longest + 1:]
    return result.at[tuple(index_at)].set(smallest).at[tuple(beside)].set(high)


def setup_inputs(seed: int = 0) -> dict:
    keys = jax.random.split(jax.random.key(seed), 6)
    teacher = draw_teacher(jax.random.fold_in(keys[5], 71), 0)
    students = draw_students(jax.random.fold_in(keys[5], 71), 0)
    prototypes = draw_prototypes(jax.random.fold_in(keys[5], 71), 0)
    pairing = place_ends(jax.random.randint(keys[3], (STUDENTS,), 0, TEA_DEV), jax.random.fold_in(keys[3], 1), 0, TEA_DEV - 1).astype(jnp.int32)
    layout = draw_layout(jax.random.fold_in(keys[5], 71), 0)
    return {"teacher": teacher, "students": students, "prototypes": prototypes, "pairing": pairing, "layout": layout}


epsilon = 1e-06
teacher_temp = 0.07
student_temp = 0.1
loss_scale = 16.0

def reference(teacher, students, prototypes, pairing, layout):
    weights = prototypes.astype(jnp.float32)
    w_norm = jnp.sqrt(lax.optimization_barrier(jnp.sum(weights * weights, 0)) + epsilon)
    w_unit = weights / w_norm
    w_unit_b = w_unit.astype(jnp.bfloat16)
    tea_full = teacher.astype(jnp.float32)
    tea_unit_b = (tea_full / jnp.sqrt(lax.optimization_barrier(jnp.sum(tea_full * tea_full, 1, keepdims=True)) + epsilon)).astype(jnp.bfloat16)
    tea_block = 256 if TEACHERS % 256 == 0 else TEACHERS
    tea_blocks = tea_unit_b.reshape(TEACHERS // tea_block, tea_block, D)

    def exp_scores(rows_b):
        return jnp.exp(jnp.dot(rows_b, w_unit_b, preferred_element_type=jnp.float32) / teacher_temp)
    row_factor = jnp.ones((TEACHERS,), jnp.float32)
    col_factor = jnp.ones((PROTOS,), jnp.float32)
    for sweep in range(ITERS):

        def add_columns(running, pieces):
            rows_b, factor = pieces
            return (running + lax.optimization_barrier(jnp.sum(exp_scores(rows_b) * factor[:, None], 0)), None)
        colsum, _ = lax.scan(add_columns, jnp.zeros((PROTOS,), jnp.float32), (tea_blocks, row_factor.reshape(-1, tea_block)))
        col_factor = 1.0 / (PROTOS * colsum)
        current = col_factor

        def row_total(rows_b):
            return lax.optimization_barrier(jnp.sum(exp_scores(rows_b) * current[None, :], 1))
        rowsum = lax.map(row_total, tea_blocks).reshape(-1)
        row_factor = 1.0 / (TEACHERS * rowsum)
    row_of = (layout * TEA_DEV + pairing).astype(jnp.int32)
    stu_full = students.astype(jnp.float32)
    u_norm = jnp.sqrt(lax.optimization_barrier(jnp.sum(stu_full * stu_full, 1, keepdims=True)) + epsilon)
    stu_unit = stu_full / u_norm
    stu_unit_b = stu_unit.astype(jnp.bfloat16)
    stu_block = 256 if STUDENTS % 256 == 0 else STUDENTS
    blocks = STUDENTS // stu_block

    def student_step(grad_w_unit, pieces):
        unit_rows, unit_rows_b, norm_rows, row_ids = pieces
        logits = jnp.dot(unit_rows_b, w_unit_b, preferred_element_type=jnp.float32) / student_temp
        exp_logits = jnp.exp(logits)
        denominator = lax.optimization_barrier(jnp.sum(exp_logits, 1, keepdims=True))
        paired = tea_unit_b[row_ids]
        target_rows = TEACHERS * exp_scores(paired) * row_factor[row_ids][:, None] * col_factor[None, :]
        grad_logits = (loss_scale / student_temp * (exp_logits / denominator - target_rows)).astype(jnp.bfloat16)
        grad_unit = jnp.dot(grad_logits, w_unit_b.T, preferred_element_type=jnp.float32)
        grad_rows = (grad_unit - unit_rows * lax.optimization_barrier(jnp.sum(unit_rows * grad_unit, 1, keepdims=True))) / norm_rows
        grad_w_unit = grad_w_unit + jnp.dot(unit_rows_b.T, grad_logits, preferred_element_type=jnp.float32)
        return (grad_w_unit, grad_rows)
    grad_w_unit, grad_blocks = lax.scan(student_step, jnp.zeros((D, PROTOS), jnp.float32), (stu_unit.reshape(blocks, stu_block, D), stu_unit_b.reshape(blocks, stu_block, D), u_norm.reshape(blocks, stu_block, 1), row_of.reshape(blocks, stu_block)))
    grad_students = grad_blocks.reshape(STUDENTS, D)
    grad_protos = (grad_w_unit - w_unit * lax.optimization_barrier(jnp.sum(w_unit * grad_w_unit, 0))) / w_norm
    return (grad_students, grad_protos)
```

```python
import functools

import jax
import jax.numpy as jnp
from jax import lax
from jax.experimental import pallas as pl
from jax.experimental.pallas import tpu as pltpu
from jax.sharding import PartitionSpec as P

F32 = jnp.float32
BF = jnp.bfloat16
MESH = pl.DeviceIdType.MESH

epsilon = 1e-06
teacher_temp = 0.07
student_temp = 0.1
loss_scale = 16.0

NT = (((1,), (1,)), ((), ()))
TN = (((0,), (0,)), ((), ()))


def dot(a, b):
    return jnp.dot(a, b, preferred_element_type=F32)


def dotg(a, b, dims):
    return lax.dot_general(a, b, dims, preferred_element_type=F32)


def iota(shape, dim):
    return lax.broadcasted_iota(jnp.int32, shape, dim)


def to_col(row, n):
    eye = iota((n, n), 0) == iota((n, n), 1)
    return jnp.sum(jnp.where(eye, jnp.broadcast_to(row, (n, n)), 0.0), 1, keepdims=True)


def to_row(col, n):
    eye = iota((n, n), 0) == iota((n, n), 1)
    return jnp.sum(jnp.where(eye, jnp.broadcast_to(col, (n, n)), 0.0), 0, keepdims=True)


def lane_fold(x):
    total = x[:, 0:128]
    for k in range(1, x.shape[1] // 128):
        total = total + x[:, k * 128:(k + 1) * 128]
    return total


class Refs:
    pass


def plan(NR, NP, T, S, D, CL):
    Z = NR // 4
    CZ = CL // Z
    B = S // NR
    FB = D // NR
    RB = S // NP
    shapes = dict(
        tq=((Z, T, D), BF),
        sb=((S, D), BF),
        pt=((S, S), F32),
        ssort=((4, S // 4, D), BF),
        msort=((4, 1, 128), F32),
        stu=((Z, 4, S // 4, D), BF),
        meta=((Z, 4, 1, 128), F32),
        w_b=((D, CL), BF),
        wzf=((D, CZ), F32),
        wz=((D, CZ), BF),
        nz=((1, CZ), F32),
        a2=((S, CL), F32),
        t2=((S, CL), F32),
        dsrc=((1, S), F32),
        drecv=((NP - 1, 1, S), F32),
        dq=((4, 1, 128), F32),
        dm=((Z, 4, 1, 128), F32),
        e1=((Z // 2, 128, CZ), F32),
        esp=((Z // 2, 256, CZ), BF),
        cs=((2, 1, CZ), F32),
        csr=((2, 3, 1, CZ), F32),
        rs=((2, 1, Z * T), F32),
        rsr=((2, Z - 1, 1, Z * T), F32),
        rp=((2, 1, Z * T), F32),
        rpr=((2, NP - 1, 1, Z * T), F32),
        tss=((4, S // 4, D), BF),
        ts=((4, S // 4, D), BF),
        tsh=((S, D), BF),
        va=((Z, 1, CZ), F32),
        a1=((Z // 2, 512, CZ), F32),
        t1=((Z // 2, 512, CZ), F32),
        st=((Z // 2, D, 512), BF),
        idxc=((Z // 2, 512, 128), F32),
        uss=((4, 1, 128), F32),
        us=((4, 1, 128), F32),
        gu=((NP, RB, D), F32),
        gur=((NP - 1, RB, D), F32),
        gsr=((NP, RB, D), F32),
        gw=((2, 2, Z, FB, CZ), F32),
        gwr=((2, Z, FB, CZ), F32),
        gy=((Z, FB, CZ), F32),
        gyr=((Z, FB, CZ), F32),
        ins=((1, CZ), F32),
        inr=((3, 1, CZ), F32),
        go=((Z, FB, CZ), F32),
        gpr=((Z, FB, CZ), F32),
    )
    return shapes


NSEM = 128


def kernel(dims, tea_ref, stu_ref, proto_ref, lay_r, lay_c, pair_c, gs_out, gp_out, *scratch):
    NR, NP, T, S, D, CL = dims
    Z = NR // 4
    CZ = CL // Z
    B = S // NR
    RPR = 2 * B
    FB = D // NR
    RB = S // NP
    PAIRS = Z // 2
    TEACHERS = T * NR
    PROTOS = CL * NP
    GS = loss_scale / student_temp
    names = list(plan(*dims))
    m = Refs()
    for name, ref in zip(names, scratch):
        setattr(m, name, ref)
    send_sem, recv_sem = scratch[len(names):]

    r = lax.axis_index("rows")
    p = lax.axis_index("protos")
    core = lax.rem(r, 2)
    z = lax.rem(r // 2, Z)
    yl = r // (2 * Z)
    qd = yl * 2 + core

    def row(y_, z_, c_):
        return (y_ * Z + z_) * 2 + c_

    zs = [lax.rem(z + d, Z) for d in range(1, Z)]
    zdev = [(row(yl, z2, core), p) for z2 in zs]
    ps = [lax.rem(p + d, NP) for d in range(1, NP)]
    pdev = [(r, p2) for p2 in ps]
    qs, qdev = [], []
    for d in (1, 2, 3):
        c2 = 1 - core if d & 1 else core
        y2 = 1 - yl if d & 2 else yl
        qs.append(y2 * 2 + c2)
        qdev.append((row(y2, z, c2), p))

    sent = []
    counter = [0]

    def start(copies):
        handles = []
        for src, dst, dev in copies:
            i = counter[0]
            counter[0] += 1
            h = pltpu.make_async_remote_copy(
                src_ref=src, dst_ref=dst, send_sem=send_sem.at[i], recv_sem=recv_sem.at[i],
                device_id=dev, device_id_type=MESH)
            h.start()
            handles.append(h)
            sent.append(h)
        return handles

    def arrive(handles):
        for h in handles:
            h.wait_recv()

    bar = pltpu.get_barrier_semaphore()
    everyone = zdev + pdev + qdev
    for dev in everyone:
        pl.semaphore_signal(bar, inc=1, device_id=dev, device_id_type=MESH)

    te = tea_ref[...].astype(F32)
    m.tq[z] = (te / jnp.sqrt(jnp.sum(te * te, 1, keepdims=True) + epsilon)).astype(BF)
    st = stu_ref[...].astype(F32)
    m.sb[...] = (st / jnp.sqrt(jnp.sum(st * st, 1, keepdims=True) + epsilon)).astype(BF)
    lc = lay_c[...]
    lr = lay_r[...]
    same = (lc == lr) & (iota((S, S), 1) < iota((S, S), 0))
    rank = jnp.sum(jnp.where(same, 1.0, 0.0), 1, keepdims=True)
    zt = lax.rem(lc // 2, Z)
    key = ((lc // (2 * Z)) * 2 + lax.rem(lc, 2)) * Z + zt
    pos = (key * B).astype(F32) + rank
    m.pt[...] = jnp.where(iota((S, S), 1).astype(F32) == pos, 1.0, 0.0)
    idx = (lax.rem(zt, 2) * T + pair_c[...]).astype(F32)
    m.ssort[...] = dotg(m.pt[...].astype(BF), m.sb[...], TN).astype(BF).reshape(4, S // 4, D)
    isort = jnp.sum(m.pt[...] * idx, 0, keepdims=True)
    spare = jnp.zeros((1, 64), F32)
    for q in range(4):
        m.msort[q] = jnp.concatenate([isort[:, q * 64:(q + 1) * 64], spare], 1)
    m.stu[z, qd] = m.ssort[qd]
    m.meta[z, qd] = m.msort[qd]

    pl.semaphore_wait(bar, len(everyone))

    c_tea = start([(m.tq.at[z], m.tq.at[z], dev) for dev in zdev])
    c_meta = start([(m.msort.at[q], m.meta.at[z, qd], dev) for q, dev in zip(qs, qdev)])
    c_stu = start([(m.ssort.at[q], m.stu.at[z, qd], dev) for q, dev in zip(qs, qdev)])

    @pl.loop(0, CZ // 256)
    def _(i):
        c = pl.multiple_of(i * 256, 256)
        w = proto_ref[:, pl.ds(pl.multiple_of(z * CZ + c, 256), 256)].astype(F32)
        n = jnp.sqrt(jnp.sum(w * w, 0, keepdims=True) + epsilon)
        u = w / n
        m.nz[:, pl.ds(c, 256)] = n
        m.wzf[:, pl.ds(c, 256)] = u
        m.wz[:, pl.ds(c, 256)] = u.astype(BF)

    @pl.loop(0, CL // 256)
    def _(i):
        c = pl.multiple_of(i * 256, 256)
        w = proto_ref[:, pl.ds(c, 256)].astype(F32)
        n = jnp.sqrt(jnp.sum(w * w, 0, keepdims=True) + epsilon)
        m.w_b[:, pl.ds(c, 256)] = (w / n).astype(BF)

    arrive(c_meta)
    arrive(c_stu)

    zr, zl = lax.rem(z + 1, Z), lax.rem(z + Z - 1, Z)
    right, left = (row(yl, zr, core), p), (row(yl, zl, core), p)
    ring = []

    def ring_step(s):
        if ring:
            arrive(ring[-1])
        a = lax.rem(z + Z - (s - 1), Z)
        b = lax.rem(z + (s - 1), Z)
        if s < Z // 2:
            ring.append(start([(m.stu.at[a], m.stu.at[a], right), (m.stu.at[b], m.stu.at[b], left)]))
        else:
            ring.append(start([
                (m.stu.at[a, pl.ds(0, 2)], m.stu.at[a, pl.ds(0, 2)], right),
                (m.stu.at[b, pl.ds(2, 2)], m.stu.at[b, pl.ds(2, 2)], left)]))

    steps = list(range(1, Z // 2 + 1))

    def next_ring():
        if steps:
            ring_step(steps.pop(0))

    next_ring()
    c_metaz = start([(m.meta.at[z], m.meta.at[z], dev) for dev in zdev])

    m.drow = None

    def a2_step(i, acc):
        c = pl.multiple_of(i * 512, 512)
        a = jnp.exp(dot(m.sb[...], m.w_b[:, pl.ds(c, 512)]) * (1.0 / student_temp))
        m.a2[:, pl.ds(c, 512)] = a
        return acc + lane_fold(a)

    acc = lax.fori_loop(0, CL // 512, a2_step, jnp.zeros((S, 128), F32))
    m.dsrc[...] = to_row(jnp.sum(acc, 1, keepdims=True), S)
    c_den = start([(m.dsrc, m.drecv.at[d], dev) for d, dev in enumerate(pdev)])

    arrive(c_tea)
    m.cs[0] = jnp.zeros((1, CZ), F32)

    @pl.loop(0, PAIRS)
    def _(k):
        tk = m.tq[pl.ds(k * 2, 2)].reshape(2 * T, D)
        for c in range(0, CZ, 512):
            e = jnp.exp(dot(tk, m.wz[:, c:c + 512]) * (1.0 / teacher_temp))
            m.e1[k, :, c:c + 512] = e
            hi = e.astype(BF)
            m.esp[k, 0:128, c:c + 512] = hi
            m.esp[k, 128:256, c:c + 512] = (e - hi.astype(F32)).astype(BF)
            m.cs[0, :, c:c + 512] += jnp.sum(e, 0, keepdims=True)

    c_cs = start([(m.cs.at[0], m.csr.at[0, d], dev) for d, dev in enumerate(qdev)])

    for k in range(PAIRS):
        rows = jnp.broadcast_to(m.meta[z], (4, RPR, 128)).reshape(4 * RPR, 128)
        mine = iota((4, RPR, 128), 2) == iota((4, RPR, 128), 1) + k * RPR
        col = jnp.sum(jnp.where(mine.reshape(4 * RPR, 128), rows, 0.0), 1, keepdims=True)
        hot = jnp.where(iota((4 * RPR, 128), 1).astype(F32) == col, 1.0, 0.0).astype(BF)
        got = dot(hot, m.tq[2 * k:2 * k + 2].reshape(2 * T, D)).astype(BF)
        m.tss[:, k * RPR:(k + 1) * RPR, :] = got.reshape(4, RPR, D)
    m.ts[qd] = m.tss[qd]
    c_ts = start([(m.tss.at[q], m.ts.at[qd], dev) for q, dev in zip(qs, qdev)])

    next_ring()

    def col_factor(it, c_cs):
        arrive(c_cs)
        return 1.0 / (PROTOS * (m.cs[it] + m.csr[it, 0] + m.csr[it, 1] + m.csr[it, 2]))

    def send_rowsum(it, v):
        for k in range(PAIRS):
            part = lane_fold(m.e1[k] * v)
            m.rs[it, :, k * 128:(k + 1) * 128] = to_row(jnp.sum(part, 1, keepdims=True), 128)
        return start([(m.rs.at[it], m.rsr.at[it, d], dev) for d, dev in enumerate(zdev)])

    def send_rowsum_protos(it, c_rs):
        arrive(c_rs)
        total = m.rs[it]
        for d in range(Z - 1):
            total = total + m.rsr[it, d]
        m.rp[it] = total
        return start([(m.rp.at[it], m.rpr.at[it, d], dev) for d, dev in enumerate(pdev)])

    def row_factor(it, c_rp):
        arrive(c_rp)
        total = m.rp[it]
        for d in range(NP - 1):
            total = total + m.rpr[it, d]
        return 1.0 / (TEACHERS * total)

    v1 = col_factor(0, c_cs)
    c_rs = send_rowsum(0, v1)

    arrive(c_den)
    den = m.dsrc[...]
    for d in range(NP - 1):
        den = den + m.drecv[d]
    sc2 = GS / to_col(den, S)
    scs = jnp.sum(m.pt[...] * sc2, 0, keepdims=True)
    for q in range(4):
        m.dq[q] = jnp.concatenate([scs[:, q * 64:(q + 1) * 64], spare], 1)
    m.dm[z, qd] = m.dq[qd]
    c_dq = start([(m.dq.at[q], m.dm.at[z, qd], dev) for q, dev in zip(qs, qdev)])
    arrive(c_ts)
    m.tsh[...] = dot(m.pt[...].astype(BF), m.ts[...].reshape(S, D)).astype(BF)
    arrive(c_dq)
    c_dz = start([(m.dm.at[z], m.dm.at[z], dev) for dev in zdev])

    c_rp = send_rowsum_protos(0, c_rs)
    next_ring()

    def t2_range(lo, hi):
        @pl.loop(lo, hi)
        def _(i):
            c = pl.multiple_of(i * 512, 512)
            m.t2[:, pl.ds(c, 512)] = jnp.exp(dot(m.tsh[...], m.w_b[:, pl.ds(c, 512)]) * (1.0 / teacher_temp))

    t2_range(0, CL // 512)

    u1 = row_factor(0, c_rp)
    part = jnp.zeros((1, CZ), F32)
    for k in range(PAIRS):
        uc = to_col(u1[:, k * 128:(k + 1) * 128], 128)
        part = part + jnp.sum(m.e1[k] * uc, 0, keepdims=True)
    m.cs[1] = part
    c_cs = start([(m.cs.at[1], m.csr.at[1, d], dev) for d, dev in enumerate(qdev)])
    next_ring()
    v2 = col_factor(1, c_cs)
    c_rs = send_rowsum(1, v2)
    m.va[z] = v2
    c_va = start([(m.va.at[z], m.va.at[z], dev) for dev in zdev])

    while steps:
        next_ring()
    arrive(ring[-1])
    arrive(c_metaz)
    arrive(c_dz)

    def block_col(ref, k):
        rows = jnp.broadcast_to(ref[...].reshape(NR, 1, 128), (NR, RPR, 128)).reshape(512, 128)
        mine = (iota((NR, RPR, 128), 2) == iota((NR, RPR, 128), 1) + k * RPR).reshape(512, 128)
        return jnp.sum(jnp.where(mine, rows, 0.0), 1, keepdims=True)

    def layout1(k):
        sk = m.stu[:, :, pl.ds(pl.multiple_of(k * RPR, RPR), RPR), :].reshape(512, D)
        m.st[k] = sk.T
        ic = block_col(m.meta, k)
        m.idxc[k] = jnp.broadcast_to(ic, (512, 128))
        sc = block_col(m.dm, k)
        hot = jnp.where(iota((512, 128), 1).astype(F32) == ic, 1.0, 0.0).astype(BF)
        hot = jnp.concatenate([hot, hot], 1)

        @pl.loop(0, CZ // 256)
        def _(i):
            c = pl.multiple_of(i * 256, 256)
            m.a1[k, :, pl.ds(c, 256)] = jnp.exp(dot(sk, m.wz[:, pl.ds(c, 256)]) * (1.0 / student_temp)) * sc
            m.t1[k, :, pl.ds(c, 256)] = dot(hot, m.esp[k, :, pl.ds(c, 256)])

    for k in range(PAIRS // 2):
        layout1(k)
    c_rp = send_rowsum_protos(1, c_rs)
    for k in range(PAIRS // 2, PAIRS):
        layout1(k)
    arrive(c_va)
    u2 = row_factor(1, c_rp) * (GS * TEACHERS)

    sel = [jnp.zeros((1, 128), F32)] * 4
    for k in range(PAIRS):
        uc = to_col(u2[:, k * 128:(k + 1) * 128], 128)
        lane = iota((128, 128), 1)
        span = (lane >= k * RPR) & (lane < (k + 1) * RPR)
        for q in range(4):
            hit = (iota((128, 128), 0).astype(F32) == m.meta[z, q]) & span
            sel[q] = sel[q] + jnp.sum(jnp.where(hit, uc, 0.0), 0, keepdims=True)
    for q in range(4):
        m.uss[q] = sel[q]
    m.us[qd] = m.uss[qd]
    c_us = start([(m.uss.at[q], m.us.at[qd], dev) for q, dev in zip(qs, qdev)])
    arrive(c_us)

    urow = jnp.concatenate([m.us[q][:, 0:64] for q in range(4)], 1)
    ucol = jnp.sum(m.pt[...] * urow, 1, keepdims=True)
    sc2 = GS / to_col(den, S)

    def g2_step(i, acc):
        c = pl.multiple_of(i * 512, 512)
        zi = i // (CZ // 512)
        vv = m.va[zi, :, pl.ds(pl.multiple_of(c - zi * CZ, 512), 512)]
        g = (m.a2[:, pl.ds(c, 512)] * sc2 - m.t2[:, pl.ds(c, 512)] * vv * ucol).astype(BF)
        return acc + dotg(g, m.w_b[:, pl.ds(c, 512)], NT)

    gsum = lax.fori_loop(0, CL // 512, g2_step, jnp.zeros((S, D), F32))
    m.gu[...] = gsum.reshape(NP, RB, D)
    c_gu = start([(m.gu.at[p2], m.gur.at[d], dev) for d, (p2, dev) in enumerate(zip(ps, pdev))])

    ucs = []
    for k in range(PAIRS):
        hit = iota((512, 128), 1).astype(F32) == m.idxc[k]
        ucs.append(jnp.sum(jnp.where(hit, jnp.broadcast_to(u2[:, k * 128:(k + 1) * 128], (512, 128)), 0.0), 1, keepdims=True))

    for c in range(0, CZ, 256):
        vv = m.va[z, :, c:c + 256]
        total = None
        for k in range(PAIRS):
            g = (m.a1[k, :, c:c + 256] - m.t1[k, :, c:c + 256] * vv * ucs[k]).astype(BF)
            one = dot(m.st[k], g)
            total = one if total is None else total + one
        m.ins[:, c:c + 256] = jnp.sum(m.wzf[:, c:c + 256] * total, 0, keepdims=True)
        for y_ in range(2):
            for z_ in range(Z):
                for c_ in range(2):
                    f = ((y_ * Z + z_) * 2 + c_) * FB
                    m.gw[c_, y_, z_, :, c:c + 256] = total[f:f + FB, :]

    c_gw = start([(m.gw.at[1 - core], m.gwr, qdev[0])])
    c_in = start([(m.ins, m.inr.at[d], dev) for d, dev in enumerate(qdev)])

    arrive(c_gu)
    gsum = m.gu[p]
    for d in range(NP - 1):
        gsum = gsum + m.gur[d]
    su = stu_ref[pl.ds(pl.multiple_of(p * RB, RB), RB), :].astype(F32)
    un = jnp.sqrt(jnp.sum(su * su, 1, keepdims=True) + epsilon)
    su = su / un
    m.gsr[p] = (gsum - su * jnp.sum(su * gsum, 1, keepdims=True)) / un
    c_gs = start([(m.gsr.at[p], m.gsr.at[p], dev) for dev in pdev])

    arrive(c_gw)
    m.gy[...] = m.gw[core, 1 - yl] + m.gwr[1 - yl]
    c_gy = start([(m.gy, m.gyr, qdev[1])])
    mine = m.gw[core, yl] + m.gwr[yl]
    arrive(c_in)
    inner = m.ins[...] + m.inr[0] + m.inr[1] + m.inr[2]
    arrive(c_gy)
    inv = 1.0 / m.nz[...]
    for z_ in range(Z):
        f = pl.multiple_of(row(yl, z_, core) * FB, FB)
        m.go[z_] = (mine[z_] + m.gyr[z_] - m.wzf[pl.ds(f, FB), :] * inner) * inv
    m.gpr[z] = m.go[z]
    c_gp = start([(m.go.at[z2], m.gpr.at[z], dev) for z2, dev in zip(zs, zdev)])
    arrive(c_gs)
    gs_out[...] = m.gsr[...].reshape(S, D)
    arrive(c_gp)
    for z_ in range(Z):
        gp_out[:, z_ * CZ:(z_ + 1) * CZ] = m.gpr[z_]
    for h in sent:
        h.wait_send()


def body(teacher, students, prototypes, pairing, layout):
    NR = lax.axis_size("rows")
    NP = lax.axis_size("protos")
    T, D = teacher.shape
    S = students.shape[0]
    CL = prototypes.shape[1]
    dims = (NR, NP, T, S, D, CL)
    vmem = pl.BlockSpec(memory_space=pltpu.VMEM)
    scratch = [pltpu.VMEM(shape, dtype) for shape, dtype in plan(*dims).values()]
    scratch += [pltpu.SemaphoreType.DMA((NSEM,)), pltpu.SemaphoreType.DMA((NSEM,))]
    return pl.pallas_call(
        functools.partial(kernel, dims),
        out_shape=(
            jax.ShapeDtypeStruct((S, D), F32),
            jax.ShapeDtypeStruct((D // NR, CL), F32),
        ),
        in_specs=[vmem] * 6,
        out_specs=(vmem, vmem),
        scratch_shapes=scratch,
        compiler_params=pltpu.CompilerParams(
            collective_id=0, has_side_effects=True, vmem_limit_bytes=62 * 1024 * 1024
        ),
        name="distill",
    )(teacher, students, prototypes, layout.reshape(1, S), layout.reshape(S, 1), pairing.reshape(S, 1))


def solution(mesh):
    in_specs = (P("rows", None), P("rows", None), P(None, "protos"), P("rows"), P("rows"))
    out_specs = (P("rows", None), P("rows", "protos"))
    return jax.shard_map(body, mesh=mesh, in_specs=in_specs, out_specs=out_specs, check_vma=False)
```

```python
import functools

import jax
import jax.numpy as jnp
from jax import lax
from jax.experimental import pallas as pl
from jax.experimental.pallas import tpu as pltpu
from jax.sharding import PartitionSpec as P

F32 = jnp.float32
BF = jnp.bfloat16
MESH = pl.DeviceIdType.MESH

epsilon = 1e-06
teacher_temp = 0.07
student_temp = 0.1
loss_scale = 16.0

NT = (((1,), (1,)), ((), ()))
TN = (((0,), (0,)), ((), ()))


def dot(a, b):
    return jnp.dot(a, b, preferred_element_type=F32)


def dotg(a, b, dims):
    return lax.dot_general(a, b, dims, preferred_element_type=F32)


def iota(shape, dim):
    return lax.broadcasted_iota(jnp.int32, shape, dim)


def to_col(row, n):
    eye = iota((n, n), 0) == iota((n, n), 1)
    return jnp.sum(jnp.where(eye, jnp.broadcast_to(row, (n, n)), 0.0), 1, keepdims=True)


def to_row(col, n):
    eye = iota((n, n), 0) == iota((n, n), 1)
    return jnp.sum(jnp.where(eye, jnp.broadcast_to(col, (n, n)), 0.0), 0, keepdims=True)


def lane_fold(x):
    total = x[:, 0:128]
    for k in range(1, x.shape[1] // 128):
        total = total + x[:, k * 128:(k + 1) * 128]
    return total


class Refs:
    pass


def plan(NR, NP, T, S, D, CL):
    Z = NR // 4
    CZ = CL // Z
    CQ = CL // 4
    FB = D // NR
    RB = S // NP
    PLANE = 4 * NP - 1
    shapes = dict(
        pr=((D, CL), BF),
        tp=((4, T, D), BF),
        tq=((Z, T, D), BF),
        sb=((S, D), BF),
        pt=((S, S), F32),
        ssort=((4, S // 4, D), BF),
        msort=((4, 1, 128), F32),
        stu=((Z, 4, S // 4, D), BF),
        meta=((Z, 4, 1, 128), F32),
        w_b=((D, CL), BF),
        wzf=((D, CZ), F32),
        wz=((D, CZ), BF),
        nz=((1, CZ), F32),
        a2=((S, CL), F32),
        t2=((S, CL), F32),
        dsrc=((1, S), F32),
        drecv=((NP - 1, 1, S), F32),
        dq=((4, 1, 128), F32),
        dm=((Z, 4, 1, 128), F32),
        e8=((4 * T, CQ), F32),
        esp=((Z // 2, 256, CZ), BF),
        cs=((2, 1, CQ), F32),
        csr=((2, Z - 1, 1, CQ), F32),
        rs=((2, 1, 4 * T), F32),
        rsr=((2, PLANE, 1, 4 * T), F32),
        ua=((Z, 1, 4 * T), F32),
        tss=((4, S // 4, D), BF),
        ts=((4, S // 4, D), BF),
        tsh=((S, D), BF),
        va=((4, 1, CQ), F32),
        a1=((Z // 2, 512, CZ), F32),
        t1=((Z // 2, 512, CZ), F32),
        st=((Z // 2, D, 512), BF),
        idxc=((Z // 2, 512, 128), F32),
        gu=((NP, RB, D), F32),
        gur=((NP - 1, RB, D), F32),
        gsr=((NP, RB, D), F32),
        gw=((2, 2, 2, Z, FB, CZ // 2), F32),
        gwr=((2, 2, Z, FB, CZ // 2), F32),
        gy=((2, Z, FB, CZ // 2), F32),
        gyr=((2, Z, FB, CZ // 2), F32),
        ins=((2, 1, CZ // 2), F32),
        inr=((2, 3, 1, CZ // 2), F32),
        go=((2, Z, FB, CZ // 2), F32),
        gpr=((2, Z, FB, CZ // 2), F32),
    )
    return shapes


NSEM = 192


def kernel(dims, tea_ref, stu_ref, proto_ref, lay_ref, pair_ref, gs_out, gp_out, *scratch):
    NR, NP, T, S, D, CL = dims
    Z = NR // 4
    CZ = CL // Z
    CQ = CL // 4
    CH = CZ // 2
    B = S // NR
    RPR = 2 * B
    FB = D // NR
    RB = S // NP
    PAIRS = Z // 2
    TEACHERS = T * NR
    PROTOS = CL * NP
    GS = loss_scale / student_temp
    names = list(plan(*dims))
    m = Refs()
    for name, ref in zip(names, scratch):
        setattr(m, name, ref)
    send_sem, recv_sem, local_sem = scratch[len(names):]

    load = pltpu.make_async_copy(proto_ref, m.pr, local_sem)
    load.start()

    r = lax.axis_index("rows")
    p = lax.axis_index("protos")
    core = lax.rem(r, 2)
    z = lax.rem(r // 2, Z)
    yl = r // (2 * Z)
    qd = yl * 2 + core

    def row(y_, z_, c_):
        return (y_ * Z + z_) * 2 + c_

    zs = [lax.rem(z + d, Z) for d in range(1, Z)]
    zdev = [(row(yl, z2, core), p) for z2 in zs]
    ps = [lax.rem(p + d, NP) for d in range(1, NP)]
    pdev = [(r, p2) for p2 in ps]
    qs, qdev = [], []
    for d in (1, 2, 3):
        c2 = 1 - core if d & 1 else core
        y2 = 1 - yl if d & 2 else yl
        qs.append(y2 * 2 + c2)
        qdev.append((row(y2, z, c2), p))
    plane = pdev + qdev + [(r2, p2) for r2, _ in qdev for p2 in ps]

    sent = []
    counter = [0]

    def start(copies):
        handles = []
        for src, dst, dev in copies:
            i = counter[0]
            counter[0] += 1
            h = pltpu.make_async_remote_copy(
                src_ref=src, dst_ref=dst, send_sem=send_sem.at[i], recv_sem=recv_sem.at[i],
                device_id=dev, device_id_type=MESH)
            h.start()
            handles.append(h)
            sent.append(h)
        return handles

    def arrive(handles):
        for h in handles:
            h.wait_recv()

    bar = pltpu.get_barrier_semaphore()
    everyone = zdev + plane
    for dev in everyone:
        pl.semaphore_signal(bar, inc=1, device_id=dev, device_id_type=MESH)

    te = tea_ref[...].astype(F32)
    te = (te / jnp.sqrt(jnp.sum(te * te, 1, keepdims=True) + epsilon)).astype(BF)
    m.tp[qd] = te
    m.tq[z] = te
    pl.semaphore_wait(bar, len(everyone))
    c_tp = start([(m.tp.at[qd], m.tp.at[qd], dev) for dev in qdev])

    st = stu_ref[...].astype(F32)
    m.sb[...] = (st / jnp.sqrt(jnp.sum(st * st, 1, keepdims=True) + epsilon)).astype(BF)
    lrf = lay_ref[...].astype(F32)
    lcf = to_col(lrf, S)
    same = (lcf == lrf) & (iota((S, S), 1) < iota((S, S), 0))
    rank = jnp.sum(jnp.where(same, 1.0, 0.0), 1, keepdims=True)
    lc = lcf.astype(jnp.int32)
    zt = lax.rem(lc // 2, Z)
    key = ((lc // (2 * Z)) * 2 + lax.rem(lc, 2)) * Z + zt
    pos = (key * B).astype(F32) + rank
    m.pt[...] = jnp.where(iota((S, S), 1).astype(F32) == pos, 1.0, 0.0)
    idx = (lax.rem(zt, 2) * T).astype(F32) + to_col(pair_ref[...].astype(F32), S)
    m.ssort[...] = dotg(m.pt[...].astype(BF), m.sb[...], TN).astype(BF).reshape(4, S // 4, D)
    isort = jnp.sum(m.pt[...] * idx, 0, keepdims=True)
    spare = jnp.zeros((1, 64), F32)
    for q in range(4):
        m.msort[q] = jnp.concatenate([isort[:, q * 64:(q + 1) * 64], spare], 1)
    m.stu[z, qd] = m.ssort[qd]
    m.meta[z, qd] = m.msort[qd]

    c_meta = start([(m.msort.at[q], m.meta.at[z, qd], dev) for q, dev in zip(qs, qdev)])
    c_stu = start([(m.ssort.at[q], m.stu.at[z, qd], dev) for q, dev in zip(qs, qdev)])
    load.wait()

    def unit(c):
        w = m.pr[:, pl.ds(pl.multiple_of(c, 256), 256)].astype(F32)
        n = jnp.sqrt(jnp.sum(w * w, 0, keepdims=True) + epsilon)
        return w / n, n

    def unit_range(lo, hi):
        @pl.loop(lo, hi)
        def _(i):
            c = pl.multiple_of(i * 256, 256)
            m.w_b[:, pl.ds(c, 256)] = unit(c)[0].astype(BF)

    base = pl.multiple_of(qd * CQ, CQ)
    unit_range(qd * (CQ // 256), (qd + 1) * (CQ // 256))

    arrive(c_tp)
    c_tea = start([(m.tq.at[z], m.tq.at[z], dev) for dev in zdev])

    @pl.loop(0, CQ // 256)
    def _(i):
        c = pl.multiple_of(i * 256, 256)
        e = jnp.exp(dot(m.tp[...].reshape(4 * T, D), m.w_b[:, pl.ds(base + c, 256)]) * (1.0 / teacher_temp))
        m.e8[:, pl.ds(c, 256)] = e
        m.cs[0, :, pl.ds(c, 256)] = jnp.sum(e, 0, keepdims=True)

    c_cs = start([(m.cs.at[0], m.csr.at[0, d], dev) for d, dev in enumerate(zdev)])

    def col_factor(it, c_cs):
        arrive(c_cs)
        total = m.cs[it]
        for d in range(Z - 1):
            total = total + m.csr[it, d]
        return 1.0 / (PROTOS * total)

    def send_rowsum(it):
        acc = jnp.zeros((4 * T, 128), F32)
        for c in range(0, CQ, 256):
            acc = acc + lane_fold(m.e8[:, c:c + 256] * m.va[qd, :, c:c + 256])
        m.rs[it] = to_row(jnp.sum(acc, 1, keepdims=True), 4 * T)
        return start([(m.rs.at[it], m.rsr.at[it, d], dev) for d, dev in enumerate(plane)])

    def row_factor(it, c_rs):
        arrive(c_rs)
        total = m.rs[it]
        for d in range(len(plane)):
            total = total + m.rsr[it, d]
        return 1.0 / (TEACHERS * total)

    zr, zl = lax.rem(z + 1, Z), lax.rem(z + Z - 1, Z)
    right, left = (row(yl, zr, core), p), (row(yl, zl, core), p)
    ring = []

    def ring_step(s):
        if ring:
            arrive(ring[-1])
        a = lax.rem(z + Z - (s - 1), Z)
        b = lax.rem(z + (s - 1), Z)
        if s < Z // 2:
            ring.append(start([(m.stu.at[a], m.stu.at[a], right), (m.stu.at[b], m.stu.at[b], left)]))
        else:
            ring.append(start([
                (m.stu.at[a, pl.ds(0, 2)], m.stu.at[a, pl.ds(0, 2)], right),
                (m.stu.at[b, pl.ds(2, 2)], m.stu.at[b, pl.ds(2, 2)], left)]))

    steps = list(range(1, Z // 2 + 1))

    def next_ring():
        if steps:
            ring_step(steps.pop(0))

    arrive(c_meta)
    arrive(c_stu)
    unit_range(0, qd * (CQ // 256))
    unit_range((qd + 1) * (CQ // 256), CL // 256)

    v1 = col_factor(0, c_cs)
    m.va[qd] = v1
    c_rs = send_rowsum(0)
    next_ring()
    c_metaz = start([(m.meta.at[z], m.meta.at[z], dev) for dev in zdev])

    def a2_step(i, acc):
        c = pl.multiple_of(i * 512, 512)
        a = jnp.exp(dot(m.sb[...], m.w_b[:, pl.ds(c, 512)]) * (1.0 / student_temp))
        m.a2[:, pl.ds(c, 512)] = a
        return acc + lane_fold(a)

    acc = lax.fori_loop(0, CL // 512, a2_step, jnp.zeros((S, 128), F32))
    m.dsrc[...] = to_row(jnp.sum(acc, 1, keepdims=True), S)
    c_den = start([(m.dsrc, m.drecv.at[d], dev) for d, dev in enumerate(pdev)])
    arrive(c_tea)

    for k in range(PAIRS):
        rows = jnp.broadcast_to(m.meta[z], (4, RPR, 128)).reshape(4 * RPR, 128)
        mine = iota((4, RPR, 128), 2) == iota((4, RPR, 128), 1) + k * RPR
        col = jnp.sum(jnp.where(mine.reshape(4 * RPR, 128), rows, 0.0), 1, keepdims=True)
        hot = jnp.where(iota((4 * RPR, 128), 1).astype(F32) == col, 1.0, 0.0).astype(BF)
        got = dot(hot, m.tq[2 * k:2 * k + 2].reshape(2 * T, D)).astype(BF)
        m.tss[:, k * RPR:(k + 1) * RPR, :] = got.reshape(4, RPR, D)
    m.ts[qd] = m.tss[qd]
    c_ts = start([(m.tss.at[q], m.ts.at[qd], dev) for q, dev in zip(qs, qdev)])

    u1 = row_factor(0, c_rs)
    uc1 = to_col(u1, 4 * T)
    for c in range(0, CQ, 256):
        m.cs[1, :, c:c + 256] = jnp.sum(m.e8[:, c:c + 256] * uc1, 0, keepdims=True)
    c_cs = start([(m.cs.at[1], m.csr.at[1, d], dev) for d, dev in enumerate(zdev)])
    next_ring()

    arrive(c_den)
    den = m.dsrc[...]
    for d in range(NP - 1):
        den = den + m.drecv[d]
    sc2 = GS / to_col(den, S)
    scs = jnp.sum(m.pt[...] * sc2, 0, keepdims=True)
    for q in range(4):
        m.dq[q] = jnp.concatenate([scs[:, q * 64:(q + 1) * 64], spare], 1)
    m.dm[z, qd] = m.dq[qd]
    c_dq = start([(m.dq.at[q], m.dm.at[z, qd], dev) for q, dev in zip(qs, qdev)])

    arrive(c_ts)
    m.tsh[...] = dot(m.pt[...].astype(BF), m.ts[...].reshape(S, D)).astype(BF)

    def t2_range(lo, hi):
        @pl.loop(lo, hi)
        def _(i):
            c = pl.multiple_of(i * 512, 512)
            m.t2[:, pl.ds(c, 512)] = jnp.exp(dot(m.tsh[...], m.w_b[:, pl.ds(c, 512)]) * (1.0 / teacher_temp))

    t2_range(0, CL // 512)
    arrive(c_dq)
    c_dz = start([(m.dm.at[z], m.dm.at[z], dev) for dev in zdev])

    v2 = col_factor(1, c_cs)
    m.va[qd] = v2
    c_rs = send_rowsum(1)
    c_va = start([(m.va.at[qd], m.va.at[qd], dev) for dev in qdev])
    next_ring()

    zbase = pl.multiple_of(z * CZ, CZ)

    @pl.loop(0, CZ // 256)
    def _(i):
        c = pl.multiple_of(i * 256, 256)
        w, n = unit(zbase + c)
        m.nz[:, pl.ds(c, 256)] = n
        m.wzf[:, pl.ds(c, 256)] = w
        m.wz[:, pl.ds(c, 256)] = w.astype(BF)

    @pl.loop(0, PAIRS)
    def _(k):
        tk = m.tq[pl.ds(k * 2, 2)].reshape(2 * T, D)
        for c in range(0, CZ, 512):
            e = jnp.exp(dot(tk, m.wz[:, c:c + 512]) * (1.0 / teacher_temp))
            hi = e.astype(BF)
            m.esp[k, 0:128, c:c + 512] = hi
            m.esp[k, 128:256, c:c + 512] = (e - hi.astype(F32)).astype(BF)

    def block_col(ref, k):
        rows = jnp.broadcast_to(ref[...].reshape(NR, 1, 128), (NR, RPR, 128)).reshape(512, 128)
        mine = (iota((NR, RPR, 128), 2) == iota((NR, RPR, 128), 1) + k * RPR).reshape(512, 128)
        return jnp.sum(jnp.where(mine, rows, 0.0), 1, keepdims=True)

    def layout1(k):
        sk = m.stu[:, :, pl.ds(pl.multiple_of(k * RPR, RPR), RPR), :].reshape(512, D)
        m.st[k] = sk.T
        ic = block_col(m.meta, k)
        m.idxc[k] = jnp.broadcast_to(ic, (512, 128))
        sc = block_col(m.dm, k)
        hot = jnp.where(iota((512, 128), 1).astype(F32) == ic, 1.0, 0.0).astype(BF)
        hot = jnp.concatenate([hot, hot], 1)

        @pl.loop(0, CZ // 256)
        def _(i):
            c = pl.multiple_of(i * 256, 256)
            m.a1[k, :, pl.ds(c, 256)] = jnp.exp(dot(sk, m.wz[:, pl.ds(c, 256)]) * (1.0 / student_temp)) * sc
            m.t1[k, :, pl.ds(c, 256)] = dot(hot, m.esp[k, :, pl.ds(c, 256)])

    u2 = row_factor(1, c_rs)
    m.ua[z] = u2 * (GS * TEACHERS)
    c_ua = start([(m.ua.at[z], m.ua.at[z], dev) for dev in zdev])
    while steps:
        next_ring()
    arrive(ring[-1])
    arrive(c_metaz)
    arrive(c_dz)
    for k in range(PAIRS):
        layout1(k)
    arrive(c_va)
    arrive(c_ua)

    def quarter(z_, q):
        return m.ua[z_, :, q * T:(q + 1) * T]

    def own(z_):
        total = None
        for q in range(4):
            one = jnp.where(qd == q, quarter(z_, q), 0.0)
            total = one if total is None else total + one
        return total

    lane = iota((512, 128), 1).astype(F32)
    ucs = []
    for k in range(PAIRS):
        urow = jnp.concatenate([own(2 * k), own(2 * k + 1)], 1)
        ucs.append(jnp.sum(jnp.where(lane == m.idxc[k], jnp.broadcast_to(urow, (512, 128)), 0.0), 1, keepdims=True))

    vbase = pl.multiple_of(lax.rem(z, Z // 4) * CZ, CZ) if Z >= 4 else None

    def v_layout1(c):
        if Z >= 4:
            return m.va[z // (Z // 4), :, pl.ds(pl.multiple_of(vbase + c, 256), 256)]
        per = 4 // Z
        q = z * per + c // CQ
        return m.va[q, :, c % CQ:c % CQ + 256]

    def grad1(h):
        for c in range(h * CH, (h + 1) * CH, 256):
            vv = v_layout1(c)
            total = None
            for k in range(PAIRS):
                g = (m.a1[k, :, c:c + 256] - m.t1[k, :, c:c + 256] * vv * ucs[k]).astype(BF)
                one = dot(m.st[k], g)
                total = one if total is None else total + one
            at = c - h * CH
            m.ins[h, :, at:at + 256] = jnp.sum(m.wzf[:, c:c + 256] * total, 0, keepdims=True)
            for y_ in range(2):
                for z_ in range(Z):
                    for c_ in range(2):
                        f = ((y_ * Z + z_) * 2 + c_) * FB
                        m.gw[h, c_, y_, z_, :, at:at + 256] = total[f:f + FB, :]
        return (start([(m.gw.at[h, 1 - core], m.gwr.at[h], qdev[0])]),
                start([(m.ins.at[h], m.inr.at[h, d], dev) for d, dev in enumerate(qdev)]))

    c_gw, c_in, c_gy, c_gp = [None] * 2, [None] * 2, [None] * 2, [None] * 2
    for h in range(2):
        c_gw[h], c_in[h] = grad1(h)

    def to_y(h):
        arrive(c_gw[h])
        m.gy[h] = m.gw[h, core, 1 - yl] + m.gwr[h, 1 - yl]
        c_gy[h] = start([(m.gy.at[h], m.gyr.at[h], qdev[1])])

    to_y(0)

    usort = []
    for q in range(4):
        for z_ in range(Z):
            usort.append(jnp.broadcast_to(quarter(z_, q), (B, T)))
    usort = jnp.concatenate(usort, 0)
    prow = m.msort[0][:, 0:64]
    for q in range(1, 4):
        prow = jnp.concatenate([prow, m.msort[q][:, 0:64]], 1)
    ztrow = jnp.broadcast_to(lax.rem(lax.broadcasted_iota(jnp.int32, (1, S), 1) // B, 2).astype(F32) * T, (1, S))
    pcol = to_col(prow - ztrow, S)
    ucol = jnp.sum(jnp.where(iota((S, T), 1).astype(F32) == pcol, usort, 0.0), 1, keepdims=True)
    ucol = jnp.sum(m.pt[...] * to_row(ucol, S), 1, keepdims=True)

    def g2_step(i, acc):
        c = pl.multiple_of(i * 512, 512)
        q = (i * 512) // CQ
        w = min(512, CQ)
        if CQ >= 512:
            vv = m.va[q, :, pl.ds(pl.multiple_of(c - q * CQ, 512), 512)]
        else:
            vv = jnp.concatenate([m.va[q + j] for j in range(512 // CQ)], 1)
        g = (m.a2[:, pl.ds(c, 512)] * sc2 - m.t2[:, pl.ds(c, 512)] * vv * ucol).astype(BF)
        return acc + dotg(g, m.w_b[:, pl.ds(c, 512)], NT)

    gsum = lax.fori_loop(0, CL // 1024, g2_step, jnp.zeros((S, D), F32))
    to_y(1)
    gsum = lax.fori_loop(CL // 1024, CL // 512, g2_step, gsum)
    m.gu[...] = gsum.reshape(NP, RB, D)
    c_gu = start([(m.gu.at[p2], m.gur.at[d], dev) for d, (p2, dev) in enumerate(zip(ps, pdev))])

    def to_z(h):
        arrive(c_in[h])
        inner = m.ins[h] + m.inr[h, 0] + m.inr[h, 1] + m.inr[h, 2]
        arrive(c_gy[h])
        inv = 1.0 / m.nz[:, h * CH:(h + 1) * CH]
        for z_ in range(Z):
            f = pl.multiple_of(row(yl, z_, core) * FB, FB)
            mine = m.gw[h, core, yl, z_] + m.gwr[h, yl, z_] + m.gyr[h, z_]
            m.go[h, z_] = (mine - m.wzf[pl.ds(f, FB), h * CH:(h + 1) * CH] * inner) * inv
        m.gpr[h, z] = m.go[h, z]
        c_gp[h] = start([(m.go.at[h, z2], m.gpr.at[h, z], dev) for z2, dev in zip(zs, zdev)])

    to_z(0)
    to_z(1)

    arrive(c_gu)
    gsum = m.gu[p]
    for d in range(NP - 1):
        gsum = gsum + m.gur[d]
    su = stu_ref[pl.ds(pl.multiple_of(p * RB, RB), RB), :].astype(F32)
    un = jnp.sqrt(jnp.sum(su * su, 1, keepdims=True) + epsilon)
    su = su / un
    m.gsr[p] = (gsum - su * jnp.sum(su * gsum, 1, keepdims=True)) / un
    c_gs = start([(m.gsr.at[p], m.gsr.at[p], dev) for dev in pdev])

    for h in range(2):
        arrive(c_gp[h])
        for z_ in range(Z):
            c = z_ * CZ + h * CH
            gp_out[:, c:c + CH] = m.gpr[h, z_]
    arrive(c_gs)
    gs_out[...] = m.gsr[...].reshape(S, D)
    for h in sent:
        h.wait_send()


def body(teacher, students, prototypes, pairing, layout):
    NR = lax.axis_size("rows")
    NP = lax.axis_size("protos")
    T, D = teacher.shape
    S = students.shape[0]
    CL = prototypes.shape[1]
    dims = (NR, NP, T, S, D, CL)
    vmem = pl.BlockSpec(memory_space=pltpu.VMEM)
    scratch = [pltpu.VMEM(shape, dtype) for shape, dtype in plan(*dims).values()]
    scratch += [pltpu.SemaphoreType.DMA((NSEM,)), pltpu.SemaphoreType.DMA((NSEM,)), pltpu.SemaphoreType.DMA]
    return pl.pallas_call(
        functools.partial(kernel, dims),
        out_shape=(
            jax.ShapeDtypeStruct((S, D), F32),
            jax.ShapeDtypeStruct((D // NR, CL), F32),
        ),
        in_specs=[vmem, vmem, pl.BlockSpec(memory_space=pl.ANY), vmem, vmem],
        out_specs=(vmem, vmem),
        scratch_shapes=scratch,
        compiler_params=pltpu.CompilerParams(
            collective_id=0, has_side_effects=True, vmem_limit_bytes=62 * 1024 * 1024
        ),
        name="distill",
    )(teacher, students, prototypes, layout.reshape(1, S), pairing.reshape(1, S))


def solution(mesh):
    in_specs = (P("rows", None), P("rows", None), P(None, "protos"), P("rows"), P("rows"))
    out_specs = (P("rows", None), P("rows", "protos"))
    return jax.shard_map(body, mesh=mesh, in_specs=in_specs, out_specs=out_specs, check_vma=False)
```

```python
import functools

import jax
import jax.numpy as jnp
from jax import lax
from jax.experimental import pallas as pl
from jax.experimental.pallas import tpu as pltpu
from jax.sharding import PartitionSpec as P

F32 = jnp.float32
BF = jnp.bfloat16
MESH = pl.DeviceIdType.MESH

epsilon = 1e-06
teacher_temp = 0.07
student_temp = 0.1
loss_scale = 16.0

NT = (((1,), (1,)), ((), ()))
TN = (((0,), (0,)), ((), ()))


def dot(a, b):
    return jnp.dot(a, b, preferred_element_type=F32)


def dotg(a, b, dims):
    return lax.dot_general(a, b, dims, preferred_element_type=F32)


def iota(shape, dim):
    return lax.broadcasted_iota(jnp.int32, shape, dim)


def to_col(row, n):
    eye = iota((n, n), 0) == iota((n, n), 1)
    return jnp.sum(jnp.where(eye, jnp.broadcast_to(row, (n, n)), 0.0), 1, keepdims=True)


def to_row(col, n):
    eye = iota((n, n), 0) == iota((n, n), 1)
    return jnp.sum(jnp.where(eye, jnp.broadcast_to(col, (n, n)), 0.0), 0, keepdims=True)


def lane_fold(x):
    total = x[:, 0:128]
    for k in range(1, x.shape[1] // 128):
        total = total + x[:, k * 128:(k + 1) * 128]
    return total


class Refs:
    pass


def plan(NR, NP, T, S, D, CL):
    Z = NR // 4
    CZ = CL // Z
    CQ = CL // 4
    FB = D // NR
    RB = S // NP
    PLANE = 4 * NP - 1
    shapes = dict(
        pr=((D, CL), BF),
        tp=((4, T, D), BF),
        tq=((Z, T, D), BF),
        sb=((S, D), BF),
        pt=((S, S), F32),
        ssort=((4, S // 4, D), BF),
        msort=((4, 1, 128), F32),
        stu=((Z, 4, S // 4, D), BF),
        meta=((Z, 4, 1, 128), F32),
        w_b=((D, CL), BF),
        wzf=((D, CZ), F32),
        wz=((D, CZ), BF),
        nz=((1, CZ), F32),
        a2=((S, CL), F32),
        t2=((S, CL), F32),
        dsrc=((1, S), F32),
        drecv=((NP - 1, 1, S), F32),
        dq=((4, 1, 128), F32),
        dm=((Z, 4, 1, 128), F32),
        e8=((4 * T, CQ), F32),
        esp=((Z // 2, 256, CZ), BF),
        cs=((2, 1, CQ), F32),
        csr=((2, Z - 1, 1, CQ), F32),
        rs=((2, 1, 4 * T), F32),
        rsr=((2, PLANE, 1, 4 * T), F32),
        ua=((Z, 1, 4 * T), F32),
        tss=((4, S // 4, D), BF),
        ts=((4, S // 4, D), BF),
        tsh=((S, D), BF),
        va=((4, 1, CQ), F32),
        a1=((Z // 2, 512, CZ), F32),
        t1=((Z // 2, 512, CZ), F32),
        st=((Z // 2, D, 512), BF),
        idxc=((Z // 2, 512, 128), F32),
        gu=((NP, RB, D), F32),
        gur=((NP - 1, RB, D), F32),
        gsr=((NP, RB, D), F32),
        gw=((2, 2, 2, Z, FB, CZ // 2), F32),
        gwr=((2, 2, Z, FB, CZ // 2), F32),
        gy=((2, Z, FB, CZ // 2), F32),
        gyr=((2, Z, FB, CZ // 2), F32),
        ins=((2, 1, CZ // 2), F32),
        inr=((2, 3, 1, CZ // 2), F32),
        go=((2, Z, FB, CZ // 2), F32),
        gpr=((2, Z, FB, CZ // 2), F32),
    )
    return shapes


NSEM = 192


def kernel(dims, tea_ref, stu_ref, proto_ref, lay_ref, pair_ref, gs_out, gp_out, *scratch):
    NR, NP, T, S, D, CL = dims
    Z = NR // 4
    CZ = CL // Z
    CQ = CL // 4
    CH = CZ // 2
    B = S // NR
    RPR = 2 * B
    FB = D // NR
    RB = S // NP
    PAIRS = Z // 2
    TEACHERS = T * NR
    PROTOS = CL * NP
    GS = loss_scale / student_temp
    names = list(plan(*dims))
    m = Refs()
    for name, ref in zip(names, scratch):
        setattr(m, name, ref)
    send_sem, recv_sem, local_sem = scratch[len(names):]

    load = pltpu.make_async_copy(proto_ref, m.pr, local_sem)
    load.start()

    r = lax.axis_index("rows")
    p = lax.axis_index("protos")
    core = lax.rem(r, 2)
    z = lax.rem(r // 2, Z)
    yl = r // (2 * Z)
    qd = yl * 2 + core

    def row(y_, z_, c_):
        return (y_ * Z + z_) * 2 + c_

    zs = [lax.rem(z + d, Z) for d in range(1, Z)]
    zdev = [(row(yl, z2, core), p) for z2 in zs]
    ps = [lax.rem(p + d, NP) for d in range(1, NP)]
    pdev = [(r, p2) for p2 in ps]
    qs, qdev = [], []
    for d in (1, 2, 3):
        c2 = 1 - core if d & 1 else core
        y2 = 1 - yl if d & 2 else yl
        qs.append(y2 * 2 + c2)
        qdev.append((row(y2, z, c2), p))
    plane = pdev + qdev + [(r2, p2) for r2, _ in qdev for p2 in ps]

    sent = []
    counter = [0]

    def start(copies):
        handles = []
        for src, dst, dev in copies:
            i = counter[0]
            counter[0] += 1
            h = pltpu.make_async_remote_copy(
                src_ref=src, dst_ref=dst, send_sem=send_sem.at[i], recv_sem=recv_sem.at[i],
                device_id=dev, device_id_type=MESH)
            h.start()
            handles.append(h)
            sent.append(h)
        return handles

    def arrive(handles):
        for h in handles:
            h.wait_recv()

    bar = pltpu.get_barrier_semaphore()
    everyone = zdev + plane
    for dev in everyone:
        pl.semaphore_signal(bar, inc=1, device_id=dev, device_id_type=MESH)

    te = tea_ref[...].astype(F32)
    te = (te * (1.0 / jnp.sqrt(jnp.sum(te * te, 1, keepdims=True) + epsilon))).astype(BF)
    m.tp[qd] = te
    m.tq[z] = te
    pl.semaphore_wait(bar, len(everyone))
    c_tp = start([(m.tp.at[qd], m.tp.at[qd], dev) for dev in qdev])

    load.wait()

    def unit(c):
        w = m.pr[:, pl.ds(pl.multiple_of(c, 256), 256)].astype(F32)
        n = jnp.sqrt(jnp.sum(w * w, 0, keepdims=True) + epsilon)
        return w * (1.0 / n), n

    def unit_range(lo, hi):
        @pl.loop(lo, hi)
        def _(i):
            c = pl.multiple_of(i * 256, 256)
            m.w_b[:, pl.ds(c, 256)] = unit(c)[0].astype(BF)

    base = pl.multiple_of(qd * CQ, CQ)
    unit_range(qd * (CQ // 256), (qd + 1) * (CQ // 256))

    arrive(c_tp)

    @pl.loop(0, CQ // 256)
    def _(i):
        c = pl.multiple_of(i * 256, 256)
        e = jnp.exp(dot(m.tp[...].reshape(4 * T, D), m.w_b[:, pl.ds(base + c, 256)]) * (1.0 / teacher_temp))
        m.e8[:, pl.ds(c, 256)] = e
        m.cs[0, :, pl.ds(c, 256)] = jnp.sum(e, 0, keepdims=True)

    c_cs = start([(m.cs.at[0], m.csr.at[0, d], dev) for d, dev in enumerate(zdev)])
    c_tea = start([(m.tq.at[z], m.tq.at[z], dev) for dev in zdev])
    st = stu_ref[...].astype(F32)
    m.sb[...] = (st * (1.0 / jnp.sqrt(jnp.sum(st * st, 1, keepdims=True) + epsilon))).astype(BF)
    lay = lay_ref[...]
    zt = (lay >> 1) & (Z - 1)
    key = (((lay >> (Z.bit_length())) * 2 + (lay & 1)) * Z + zt).astype(F32)
    kcol = to_col(key, S)
    same = (kcol == key) & (iota((S, S), 1) < iota((S, S), 0))
    pos = kcol * B + jnp.sum(jnp.where(same, 1.0, 0.0), 1, keepdims=True)
    m.pt[...] = jnp.where(iota((S, S), 1).astype(F32) == pos, 1.0, 0.0)
    idx = to_col(((zt & 1) * T + pair_ref[...]).astype(F32), S)
    m.ssort[...] = dotg(m.pt[...].astype(BF), m.sb[...], TN).astype(BF).reshape(4, S // 4, D)
    isort = jnp.sum(m.pt[...] * idx, 0, keepdims=True)
    spare = jnp.zeros((1, 64), F32)
    for q in range(4):
        m.msort[q] = jnp.concatenate([isort[:, q * 64:(q + 1) * 64], spare], 1)
    m.stu[z, qd] = m.ssort[qd]
    m.meta[z, qd] = m.msort[qd]

    c_meta = start([(m.msort.at[q], m.meta.at[z, qd], dev) for q, dev in zip(qs, qdev)])
    c_stu = start([(m.ssort.at[q], m.stu.at[z, qd], dev) for q, dev in zip(qs, qdev)])

    def col_factor(it, c_cs):
        arrive(c_cs)
        total = m.cs[it]
        for d in range(Z - 1):
            total = total + m.csr[it, d]
        return 1.0 / (PROTOS * total)

    def send_rowsum(it):
        acc = jnp.zeros((4 * T, 128), F32)
        for c in range(0, CQ, 256):
            acc = acc + lane_fold(m.e8[:, c:c + 256] * m.va[qd, :, c:c + 256])
        m.rs[it] = to_row(jnp.sum(acc, 1, keepdims=True), 4 * T)
        return start([(m.rs.at[it], m.rsr.at[it, d], dev) for d, dev in enumerate(plane)])

    def row_factor(it, c_rs):
        arrive(c_rs)
        total = m.rs[it]
        for d in range(len(plane)):
            total = total + m.rsr[it, d]
        return 1.0 / (TEACHERS * total)

    zr, zl = lax.rem(z + 1, Z), lax.rem(z + Z - 1, Z)
    right, left = (row(yl, zr, core), p), (row(yl, zl, core), p)
    ring = []

    def ring_step(s):
        if ring:
            arrive(ring[-1])
        a = lax.rem(z + Z - (s - 1), Z)
        b = lax.rem(z + (s - 1), Z)
        if s < Z // 2:
            ring.append(start([(m.stu.at[a], m.stu.at[a], right), (m.stu.at[b], m.stu.at[b], left)]))
        else:
            ring.append(start([
                (m.stu.at[a, pl.ds(0, 2)], m.stu.at[a, pl.ds(0, 2)], right),
                (m.stu.at[b, pl.ds(2, 2)], m.stu.at[b, pl.ds(2, 2)], left)]))

    steps = list(range(1, Z // 2 + 1))

    def next_ring():
        if steps:
            ring_step(steps.pop(0))

    unit_range(0, qd * (CQ // 256))
    unit_range((qd + 1) * (CQ // 256), CL // 256)

    v1 = col_factor(0, c_cs)
    m.va[qd] = v1
    c_rs = send_rowsum(0)
    arrive(c_meta)
    arrive(c_stu)
    next_ring()
    c_metaz = start([(m.meta.at[z], m.meta.at[z], dev) for dev in zdev])

    def a2_step(i, acc):
        c = pl.multiple_of(i * 512, 512)
        a = jnp.exp(dot(m.sb[...], m.w_b[:, pl.ds(c, 512)]) * (1.0 / student_temp))
        m.a2[:, pl.ds(c, 512)] = a
        return acc + lane_fold(a)

    acc = lax.fori_loop(0, CL // 512, a2_step, jnp.zeros((S, 128), F32))
    m.dsrc[...] = to_row(jnp.sum(acc, 1, keepdims=True), S)
    c_den = start([(m.dsrc, m.drecv.at[d], dev) for d, dev in enumerate(pdev)])
    arrive(c_tea)

    for k in range(PAIRS):
        rows = jnp.broadcast_to(m.meta[z], (4, RPR, 128)).reshape(4 * RPR, 128)
        mine = iota((4, RPR, 128), 2) == iota((4, RPR, 128), 1) + k * RPR
        col = jnp.sum(jnp.where(mine.reshape(4 * RPR, 128), rows, 0.0), 1, keepdims=True)
        hot = jnp.where(iota((4 * RPR, 128), 1).astype(F32) == col, 1.0, 0.0).astype(BF)
        got = dot(hot, m.tq[2 * k:2 * k + 2].reshape(2 * T, D)).astype(BF)
        m.tss[:, k * RPR:(k + 1) * RPR, :] = got.reshape(4, RPR, D)
    m.ts[qd] = m.tss[qd]
    c_ts = start([(m.tss.at[q], m.ts.at[qd], dev) for q, dev in zip(qs, qdev)])

    zbase = pl.multiple_of(z * CZ, CZ)

    @pl.loop(0, CZ // 256)
    def _(i):
        c = pl.multiple_of(i * 256, 256)
        w, n = unit(zbase + c)
        m.nz[:, pl.ds(c, 256)] = n
        m.wzf[:, pl.ds(c, 256)] = w
        m.wz[:, pl.ds(c, 256)] = w.astype(BF)

    u1 = row_factor(0, c_rs)
    uc1 = to_col(u1, 4 * T)
    for c in range(0, CQ, 256):
        m.cs[1, :, c:c + 256] = jnp.sum(m.e8[:, c:c + 256] * uc1, 0, keepdims=True)
    c_cs = start([(m.cs.at[1], m.csr.at[1, d], dev) for d, dev in enumerate(zdev)])
    next_ring()

    arrive(c_den)
    den = m.dsrc[...]
    for d in range(NP - 1):
        den = den + m.drecv[d]
    sc2 = GS / to_col(den, S)
    scs = jnp.sum(m.pt[...] * sc2, 0, keepdims=True)
    for q in range(4):
        m.dq[q] = jnp.concatenate([scs[:, q * 64:(q + 1) * 64], spare], 1)
    m.dm[z, qd] = m.dq[qd]
    c_dq = start([(m.dq.at[q], m.dm.at[z, qd], dev) for q, dev in zip(qs, qdev)])

    arrive(c_ts)
    m.tsh[...] = dot(m.pt[...].astype(BF), m.ts[...].reshape(S, D)).astype(BF)

    def t2_range(lo, hi):
        @pl.loop(lo, hi)
        def _(i):
            c = pl.multiple_of(i * 512, 512)
            m.t2[:, pl.ds(c, 512)] = jnp.exp(dot(m.tsh[...], m.w_b[:, pl.ds(c, 512)]) * (1.0 / teacher_temp))

    t2_range(0, CL // 512)
    arrive(c_dq)
    c_dz = start([(m.dm.at[z], m.dm.at[z], dev) for dev in zdev])

    v2 = col_factor(1, c_cs)
    m.va[qd] = v2
    c_rs = send_rowsum(1)
    c_va = start([(m.va.at[qd], m.va.at[qd], dev) for dev in qdev])
    while steps:
        next_ring()

    @pl.loop(0, PAIRS)
    def _(k):
        tk = m.tq[pl.ds(k * 2, 2)].reshape(2 * T, D)
        for c in range(0, CZ, 512):
            e = jnp.exp(dot(tk, m.wz[:, c:c + 512]) * (1.0 / teacher_temp))
            hi = e.astype(BF)
            m.esp[k, 0:128, c:c + 512] = hi
            m.esp[k, 128:256, c:c + 512] = (e - hi.astype(F32)).astype(BF)

    def block_col(ref, k):
        rows = jnp.broadcast_to(ref[...].reshape(NR, 1, 128), (NR, RPR, 128)).reshape(512, 128)
        mine = (iota((NR, RPR, 128), 2) == iota((NR, RPR, 128), 1) + k * RPR).reshape(512, 128)
        return jnp.sum(jnp.where(mine, rows, 0.0), 1, keepdims=True)

    vbase = pl.multiple_of(lax.rem(z, Z // 4) * CZ, CZ) if Z >= 4 else None

    def v_layout1(c):
        if Z >= 4:
            return m.va[z // (Z // 4), :, pl.ds(pl.multiple_of(vbase + c, 256), 256)]
        per = 4 // Z
        q = z * per + c // CQ
        return m.va[q, :, pl.ds(pl.multiple_of(c % CQ, 256), 256)]

    def layout1(k):
        sk = m.stu[:, :, pl.ds(pl.multiple_of(k * RPR, RPR), RPR), :].reshape(512, D)
        m.st[k] = sk.T
        ic = block_col(m.meta, k)
        m.idxc[k] = jnp.broadcast_to(ic, (512, 128))
        sc = block_col(m.dm, k)
        hot = jnp.where(iota((512, 128), 1).astype(F32) == ic, 1.0, 0.0).astype(BF)
        hot = jnp.concatenate([hot, hot], 1)

        @pl.loop(0, CZ // 256)
        def _(i):
            c = pl.multiple_of(i * 256, 256)
            m.a1[k, :, pl.ds(c, 256)] = jnp.exp(dot(sk, m.wz[:, pl.ds(c, 256)]) * (1.0 / student_temp)) * sc
            m.t1[k, :, pl.ds(c, 256)] = dot(hot, m.esp[k, :, pl.ds(c, 256)]) * v_layout1(c)

    arrive(c_va)
    arrive(c_metaz)
    arrive(c_dz)
    arrive(ring[-1])
    for k in range(PAIRS // 2):
        layout1(k)
    u2 = row_factor(1, c_rs)
    m.ua[z] = u2 * (GS * TEACHERS)
    c_ua = start([(m.ua.at[z], m.ua.at[z], dev) for dev in zdev])
    for k in range(PAIRS // 2, PAIRS):
        layout1(k)
    arrive(c_ua)

    def quarter(z_, q):
        return m.ua[z_, :, q * T:(q + 1) * T]

    def own(z_):
        total = None
        for q in range(4):
            one = jnp.where(qd == q, quarter(z_, q), 0.0)
            total = one if total is None else total + one
        return total

    lane = iota((512, 128), 1).astype(F32)
    ucs = []
    for k in range(PAIRS):
        urow = jnp.concatenate([own(2 * k), own(2 * k + 1)], 1)
        ucs.append(jnp.sum(jnp.where(lane == m.idxc[k], jnp.broadcast_to(urow, (512, 128)), 0.0), 1, keepdims=True))

    def grad1(h):
        for c in range(h * CH, (h + 1) * CH, 256):
            total = None
            for k in range(PAIRS):
                g = (m.a1[k, :, c:c + 256] - m.t1[k, :, c:c + 256] * ucs[k]).astype(BF)
                one = dot(m.st[k], g)
                total = one if total is None else total + one
            at = c - h * CH
            m.ins[h, :, at:at + 256] = jnp.sum(m.wzf[:, c:c + 256] * total, 0, keepdims=True)
            for y_ in range(2):
                for z_ in range(Z):
                    for c_ in range(2):
                        f = ((y_ * Z + z_) * 2 + c_) * FB
                        m.gw[h, c_, y_, z_, :, at:at + 256] = total[f:f + FB, :]
        return (start([(m.gw.at[h, 1 - core], m.gwr.at[h], qdev[0])]),
                start([(m.ins.at[h], m.inr.at[h, d], dev) for d, dev in enumerate(qdev)]))

    c_gw, c_in, c_gy, c_gp = [None] * 2, [None] * 2, [None] * 2, [None] * 2
    for h in range(2):
        c_gw[h], c_in[h] = grad1(h)

    def to_y(h):
        arrive(c_gw[h])
        m.gy[h] = m.gw[h, core, 1 - yl] + m.gwr[h, 1 - yl]
        c_gy[h] = start([(m.gy.at[h], m.gyr.at[h], qdev[1])])

    to_y(0)

    usort = []
    for q in range(4):
        for z_ in range(Z):
            usort.append(jnp.broadcast_to(quarter(z_, q), (B, T)))
    usort = jnp.concatenate(usort, 0)
    prow = m.msort[0][:, 0:64]
    for q in range(1, 4):
        prow = jnp.concatenate([prow, m.msort[q][:, 0:64]], 1)
    ztrow = jnp.broadcast_to(((iota((1, S), 1) >> (B.bit_length() - 1)) & 1).astype(F32) * T, (1, S))
    pcol = to_col(prow - ztrow, S)
    ucol = jnp.sum(jnp.where(iota((S, T), 1).astype(F32) == pcol, usort, 0.0), 1, keepdims=True)
    ucol = jnp.sum(m.pt[...] * to_row(ucol, S), 1, keepdims=True)

    def g2_step(i, acc):
        c = pl.multiple_of(i * 512, 512)
        q = (i * 512) // CQ
        w = min(512, CQ)
        if CQ >= 512:
            vv = m.va[q, :, pl.ds(pl.multiple_of(c - q * CQ, 512), 512)]
        else:
            vv = jnp.concatenate([m.va[q + j] for j in range(512 // CQ)], 1)
        g = (m.a2[:, pl.ds(c, 512)] * sc2 - m.t2[:, pl.ds(c, 512)] * vv * ucol).astype(BF)
        return acc + dotg(g, m.w_b[:, pl.ds(c, 512)], NT)

    gsum = lax.fori_loop(0, CL // 1024, g2_step, jnp.zeros((S, D), F32))
    to_y(1)
    gsum = lax.fori_loop(CL // 1024, CL // 512, g2_step, gsum)
    m.gu[...] = gsum.reshape(NP, RB, D)
    c_gu = start([(m.gu.at[p2], m.gur.at[d], dev) for d, (p2, dev) in enumerate(zip(ps, pdev))])

    def to_z(h):
        arrive(c_in[h])
        inner = m.ins[h] + m.inr[h, 0] + m.inr[h, 1] + m.inr[h, 2]
        arrive(c_gy[h])
        inv = 1.0 / m.nz[:, h * CH:(h + 1) * CH]
        for z_ in range(Z):
            f = pl.multiple_of(row(yl, z_, core) * FB, FB)
            mine = m.gw[h, core, yl, z_] + m.gwr[h, yl, z_] + m.gyr[h, z_]
            m.go[h, z_] = (mine - m.wzf[pl.ds(f, FB), h * CH:(h + 1) * CH] * inner) * inv
        m.gpr[h, z] = m.go[h, z]
        c_gp[h] = start([(m.go.at[h, z2], m.gpr.at[h, z], dev) for z2, dev in zip(zs, zdev)])

    to_z(0)
    to_z(1)

    arrive(c_gu)
    gsum = m.gu[p]
    for d in range(NP - 1):
        gsum = gsum + m.gur[d]
    su = stu_ref[pl.ds(pl.multiple_of(p * RB, RB), RB), :].astype(F32)
    un = jnp.sqrt(jnp.sum(su * su, 1, keepdims=True) + epsilon)
    su = su / un
    m.gsr[p] = (gsum - su * jnp.sum(su * gsum, 1, keepdims=True)) / un
    c_gs = start([(m.gsr.at[p], m.gsr.at[p], dev) for dev in pdev])

    for h in range(2):
        arrive(c_gp[h])
        for z_ in range(Z):
            c = z_ * CZ + h * CH
            gp_out[:, c:c + CH] = m.gpr[h, z_]
    arrive(c_gs)
    gs_out[...] = m.gsr[...].reshape(S, D)
    for h in sent:
        h.wait_send()


def body(teacher, students, prototypes, pairing, layout):
    NR = lax.axis_size("rows")
    NP = lax.axis_size("protos")
    T, D = teacher.shape
    S = students.shape[0]
    CL = prototypes.shape[1]
    dims = (NR, NP, T, S, D, CL)
    vmem = pl.BlockSpec(memory_space=pltpu.VMEM)
    scratch = [pltpu.VMEM(shape, dtype) for shape, dtype in plan(*dims).values()]
    scratch += [pltpu.SemaphoreType.DMA((NSEM,)), pltpu.SemaphoreType.DMA((NSEM,)), pltpu.SemaphoreType.DMA]
    return pl.pallas_call(
        functools.partial(kernel, dims),
        out_shape=(
            jax.ShapeDtypeStruct((S, D), F32),
            jax.ShapeDtypeStruct((D // NR, CL), F32),
        ),
        in_specs=[vmem, vmem, pl.BlockSpec(memory_space=pl.ANY), vmem, vmem],
        out_specs=(vmem, vmem),
        scratch_shapes=scratch,
        compiler_params=pltpu.CompilerParams(
            collective_id=0, has_side_effects=True, vmem_limit_bytes=62 * 1024 * 1024
        ),
        name="distill",
    )(teacher, students, prototypes, layout.reshape(1, S), pairing.reshape(1, S))


def solution(mesh):
    in_specs = (P("rows", None), P("rows", None), P(None, "protos"), P("rows"), P("rows"))
    out_specs = (P("rows", None), P("rows", "protos"))
    return jax.shard_map(body, mesh=mesh, in_specs=in_specs, out_specs=out_specs, check_vma=False)
```

```python
import functools

import jax
import jax.numpy as jnp
from jax import lax
from jax.experimental import pallas as pl
from jax.experimental.pallas import tpu as pltpu
from jax.sharding import PartitionSpec as P

F32 = jnp.float32
BF = jnp.bfloat16
MESH = pl.DeviceIdType.MESH

epsilon = 1e-06
teacher_temp = 0.07
student_temp = 0.1
loss_scale = 16.0

NT = (((1,), (1,)), ((), ()))
TN = (((0,), (0,)), ((), ()))


def dot(a, b):
    return jnp.dot(a, b, preferred_element_type=F32)


def dotg(a, b, dims):
    return lax.dot_general(a, b, dims, preferred_element_type=F32)


def iota(shape, dim):
    return lax.broadcasted_iota(jnp.int32, shape, dim)


def to_col(row, n):
    eye = iota((n, n), 0) == iota((n, n), 1)
    return jnp.sum(jnp.where(eye, jnp.broadcast_to(row, (n, n)), 0.0), 1, keepdims=True)


def to_row(col, n):
    eye = iota((n, n), 0) == iota((n, n), 1)
    return jnp.sum(jnp.where(eye, jnp.broadcast_to(col, (n, n)), 0.0), 0, keepdims=True)


def lane_fold(x):
    total = x[:, 0:128]
    for k in range(1, x.shape[1] // 128):
        total = total + x[:, k * 128:(k + 1) * 128]
    return total


class Refs:
    pass


def plan(NR, NP, T, S, D, CL):
    Z = NR // 4
    CZ = CL // Z
    CQ = CL // 4
    FB = D // NR
    RB = S // NP
    PLANE = 4 * NP - 1
    shapes = dict(
        w_b=((D, CL), BF),
        tea=((T, D), BF),
        stu_in=((S, D), BF),
        lay=((1, S), jnp.int32),
        pair=((1, S), jnp.int32),
        tp=((4, T, D), BF),
        tq=((Z, T, D), BF),
        sb=((S, D), BF),
        pt=((S, S), F32),
        ssort=((4, S // 4, D), BF),
        msort=((4, 1, 128), F32),
        stu=((Z, 4, S // 4, D), BF),
        meta=((Z, 4, 1, 128), F32),
        wzf=((D, CZ), F32),
        wz=((D, CZ), BF),
        nz=((1, CZ), F32),
        a2=((S, CL), F32),
        t2=((S, CL), F32),
        dsrc=((1, S), F32),
        drecv=((NP - 1, 1, S), F32),
        dq=((4, 1, 128), F32),
        dm=((Z, 4, 1, 128), F32),
        e8=((4 * T, CQ), F32),
        esp=((Z // 2, 256, CZ), BF),
        cs=((2, 1, CQ), F32),
        csr=((2, Z - 1, 1, CQ), F32),
        rs=((2, 1, 4 * T), F32),
        rsr=((2, PLANE, 1, 4 * T), F32),
        ua=((Z, 1, 4 * T), F32),
        tss=((4, S // 4, D), BF),
        ts=((4, S // 4, D), BF),
        tsh=((S, D), BF),
        va=((4, 1, CQ), F32),
        a1=((Z // 2, 512, CZ), F32),
        t1=((Z // 2, 512, CZ), F32),
        st=((Z // 2, D, 512), BF),
        idxc=((Z // 2, 512, 128), F32),
        gu=((NP, RB, D), F32),
        gur=((NP - 1, RB, D), F32),
        gsr=((NP, RB, D), F32),
        gw=((2, 2, 2, Z, FB, CZ // 2), F32),
        gwr=((2, 2, Z, FB, CZ // 2), F32),
        gy=((2, Z, FB, CZ // 2), F32),
        gyr=((2, Z, FB, CZ // 2), F32),
        ins=((2, 1, CZ // 2), F32),
        inr=((2, 3, 1, CZ // 2), F32),
        go=((2, Z, FB, CZ // 2), F32),
        gpr=((2, Z, FB, CZ // 2), F32),
    )
    return shapes


NSEM = 192
VMEM_MIB = 52


def kernel(dims, tea_in, stu_in, proto_ref, lay_in, pair_in, gs_out, gp_out, *scratch):
    NR, NP, T, S, D, CL = dims
    Z = NR // 4
    CZ = CL // Z
    CQ = CL // 4
    CH = CZ // 2
    B = S // NR
    RPR = 2 * B
    FB = D // NR
    RB = S // NP
    PAIRS = Z // 2
    TEACHERS = T * NR
    PROTOS = CL * NP
    GS = loss_scale / student_temp
    names = list(plan(*dims))
    m = Refs()
    for name, ref in zip(names, scratch):
        setattr(m, name, ref)
    send_sem, recv_sem, local_sem = scratch[len(names):]
    tea_ref, stu_ref, lay_ref, pair_ref = m.tea, m.stu_in, m.lay, m.pair

    load = pltpu.make_async_copy(proto_ref, m.w_b, local_sem.at[0])
    small = [
        pltpu.make_async_copy(src, dst, local_sem.at[1 + i])
        for i, (src, dst) in enumerate(((tea_in, tea_ref), (stu_in, stu_ref), (lay_in, lay_ref), (pair_in, pair_ref)))]
    for c in small:
        c.start()
    load.start()

    r = lax.axis_index("rows")
    p = lax.axis_index("protos")
    core = lax.rem(r, 2)
    z = lax.rem(r // 2, Z)
    yl = r // (2 * Z)
    qd = yl * 2 + core

    def row(y_, z_, c_):
        return (y_ * Z + z_) * 2 + c_

    zs = [lax.rem(z + d, Z) for d in range(1, Z)]
    zdev = [(row(yl, z2, core), p) for z2 in zs]
    ps = [lax.rem(p + d, NP) for d in range(1, NP)]
    pdev = [(r, p2) for p2 in ps]
    qs, qdev = [], []
    for d in (1, 2, 3):
        c2 = 1 - core if d & 1 else core
        y2 = 1 - yl if d & 2 else yl
        qs.append(y2 * 2 + c2)
        qdev.append((row(y2, z, c2), p))
    plane = pdev + qdev + [(r2, p2) for r2, _ in qdev for p2 in ps]

    sent = []
    counter = [0]

    def start(copies):
        handles = []
        for src, dst, dev in copies:
            i = counter[0]
            counter[0] += 1
            h = pltpu.make_async_remote_copy(
                src_ref=src, dst_ref=dst, send_sem=send_sem.at[i], recv_sem=recv_sem.at[i],
                device_id=dev, device_id_type=MESH)
            h.start()
            handles.append(h)
            sent.append(h)
        return handles

    def arrive(handles):
        for h in handles:
            h.wait_recv()

    bar = pltpu.get_barrier_semaphore()
    everyone = zdev + plane
    for dev in everyone:
        pl.semaphore_signal(bar, inc=1, device_id=dev, device_id_type=MESH)

    for c in small:
        c.wait()
    te = tea_ref[...].astype(F32)
    te = (te * (1.0 / jnp.sqrt(jnp.sum(te * te, 1, keepdims=True) + epsilon))).astype(BF)
    m.tp[qd] = te
    m.tq[z] = te
    pl.semaphore_wait(bar, len(everyone))
    c_tp = start([(m.tp.at[qd], m.tp.at[qd], dev) for dev in qdev])

    st = stu_ref[...].astype(F32)
    m.sb[...] = (st * (1.0 / jnp.sqrt(jnp.sum(st * st, 1, keepdims=True) + epsilon))).astype(BF)
    lay = lay_ref[...]
    zt = (lay >> 1) & (Z - 1)
    key = (((lay >> (Z.bit_length())) * 2 + (lay & 1)) * Z + zt).astype(F32)
    kcol = to_col(key, S)
    same = (kcol == key) & (iota((S, S), 1) < iota((S, S), 0))
    pos = kcol * B + jnp.sum(jnp.where(same, 1.0, 0.0), 1, keepdims=True)
    m.pt[...] = jnp.where(iota((S, S), 1).astype(F32) == pos, 1.0, 0.0)
    idx = to_col(((zt & 1) * T + pair_ref[...]).astype(F32), S)
    m.ssort[...] = dotg(m.pt[...].astype(BF), m.sb[...], TN).astype(BF).reshape(4, S // 4, D)
    isort = jnp.sum(m.pt[...] * idx, 0, keepdims=True)
    spare = jnp.zeros((1, 64), F32)
    for q in range(4):
        m.msort[q] = jnp.concatenate([isort[:, q * 64:(q + 1) * 64], spare], 1)
    m.stu[z, qd] = m.ssort[qd]
    m.meta[z, qd] = m.msort[qd]

    c_meta = start([(m.msort.at[q], m.meta.at[z, qd], dev) for q, dev in zip(qs, qdev)])
    c_stu = start([(m.ssort.at[q], m.stu.at[z, qd], dev) for q, dev in zip(qs, qdev)])

    load.wait()

    def unit(c):
        w = m.w_b[:, pl.ds(pl.multiple_of(c, 256), 256)].astype(F32)
        n = jnp.sqrt(jnp.sum(w * w, 0, keepdims=True) + epsilon)
        return w * (1.0 / n), n

    def unit_range(lo, hi):
        @pl.loop(lo, hi)
        def _(i):
            c = pl.multiple_of(i * 256, 256)
            m.w_b[:, pl.ds(c, 256)] = unit(c)[0].astype(BF)

    zbase = pl.multiple_of(z * CZ, CZ)

    @pl.loop(0, CZ // 256)
    def _(i):
        c = pl.multiple_of(i * 256, 256)
        w, n = unit(zbase + c)
        m.nz[:, pl.ds(c, 256)] = n
        m.wzf[:, pl.ds(c, 256)] = w
        m.wz[:, pl.ds(c, 256)] = w.astype(BF)

    base = pl.multiple_of(qd * CQ, CQ)
    unit_range(qd * (CQ // 256), (qd + 1) * (CQ // 256))

    arrive(c_tp)

    @pl.loop(0, CQ // 256)
    def _(i):
        c = pl.multiple_of(i * 256, 256)
        e = jnp.exp(dot(m.tp[...].reshape(4 * T, D), m.w_b[:, pl.ds(base + c, 256)]) * (1.0 / teacher_temp))
        m.e8[:, pl.ds(c, 256)] = e
        m.cs[0, :, pl.ds(c, 256)] = jnp.sum(e, 0, keepdims=True)

    c_cs = start([(m.cs.at[0], m.csr.at[0, d], dev) for d, dev in enumerate(zdev)])
    def col_factor(it, c_cs):
        arrive(c_cs)
        total = m.cs[it]
        for d in range(Z - 1):
            total = total + m.csr[it, d]
        return 1.0 / (PROTOS * total)

    def send_rowsum(it):
        acc = jnp.zeros((4 * T, 128), F32)
        for c in range(0, CQ, 256):
            acc = acc + lane_fold(m.e8[:, c:c + 256] * m.va[qd, :, c:c + 256])
        m.rs[it] = to_row(jnp.sum(acc, 1, keepdims=True), 4 * T)
        return start([(m.rs.at[it], m.rsr.at[it, d], dev) for d, dev in enumerate(plane)])

    def row_factor(it, c_rs):
        arrive(c_rs)
        total = m.rs[it]
        for d in range(len(plane)):
            total = total + m.rsr[it, d]
        return 1.0 / (TEACHERS * total)

    zr, zl = lax.rem(z + 1, Z), lax.rem(z + Z - 1, Z)
    right, left = (row(yl, zr, core), p), (row(yl, zl, core), p)
    ring = []

    def ring_step(s):
        if ring:
            arrive(ring[-1])
        a = lax.rem(z + Z - (s - 1), Z)
        b = lax.rem(z + (s - 1), Z)
        if s < Z // 2:
            ring.append(start([(m.stu.at[a], m.stu.at[a], right), (m.stu.at[b], m.stu.at[b], left)]))
        else:
            ring.append(start([
                (m.stu.at[a, pl.ds(0, 2)], m.stu.at[a, pl.ds(0, 2)], right),
                (m.stu.at[b, pl.ds(2, 2)], m.stu.at[b, pl.ds(2, 2)], left)]))

    steps = list(range(1, Z // 2 + 1))

    def next_ring():
        if steps:
            ring_step(steps.pop(0))

    arrive(c_meta)
    arrive(c_stu)
    next_ring()
    unit_range(0, qd * (CQ // 256))
    unit_range((qd + 1) * (CQ // 256), CL // 256)

    v1 = col_factor(0, c_cs)
    m.va[qd] = v1
    c_rs = send_rowsum(0)
    next_ring()
    c_tea = start([(m.tq.at[z], m.tq.at[z], dev) for dev in zdev])
    c_metaz = start([(m.meta.at[z], m.meta.at[z], dev) for dev in zdev])

    def a2_step(i, acc):
        c = pl.multiple_of(i * 512, 512)
        a = jnp.exp(dot(m.sb[...], m.w_b[:, pl.ds(c, 512)]) * (1.0 / student_temp))
        m.a2[:, pl.ds(c, 512)] = a
        return acc + lane_fold(a)

    acc = lax.fori_loop(0, CL // 512, a2_step, jnp.zeros((S, 128), F32))
    m.dsrc[...] = to_row(jnp.sum(acc, 1, keepdims=True), S)
    c_den = start([(m.dsrc, m.drecv.at[d], dev) for d, dev in enumerate(pdev)])
    arrive(c_tea)

    for k in range(PAIRS):
        rows = jnp.broadcast_to(m.meta[z], (4, RPR, 128)).reshape(4 * RPR, 128)
        mine = iota((4, RPR, 128), 2) == iota((4, RPR, 128), 1) + k * RPR
        col = jnp.sum(jnp.where(mine.reshape(4 * RPR, 128), rows, 0.0), 1, keepdims=True)
        hot = jnp.where(iota((4 * RPR, 128), 1).astype(F32) == col, 1.0, 0.0).astype(BF)
        got = dot(hot, m.tq[2 * k:2 * k + 2].reshape(2 * T, D)).astype(BF)
        m.tss[:, k * RPR:(k + 1) * RPR, :] = got.reshape(4, RPR, D)
    m.ts[qd] = m.tss[qd]
    c_ts = start([(m.tss.at[q], m.ts.at[qd], dev) for q, dev in zip(qs, qdev)])

    u1 = row_factor(0, c_rs)
    uc1 = to_col(u1, 4 * T)
    for c in range(0, CQ, 256):
        m.cs[1, :, c:c + 256] = jnp.sum(m.e8[:, c:c + 256] * uc1, 0, keepdims=True)
    c_cs = start([(m.cs.at[1], m.csr.at[1, d], dev) for d, dev in enumerate(zdev)])

    arrive(c_den)
    den = m.dsrc[...]
    for d in range(NP - 1):
        den = den + m.drecv[d]
    sc2 = GS / to_col(den, S)
    scs = jnp.sum(m.pt[...] * sc2, 0, keepdims=True)
    for q in range(4):
        m.dq[q] = jnp.concatenate([scs[:, q * 64:(q + 1) * 64], spare], 1)
    m.dm[z, qd] = m.dq[qd]
    c_dq = start([(m.dq.at[q], m.dm.at[z, qd], dev) for q, dev in zip(qs, qdev)])

    next_ring()
    arrive(c_ts)
    m.tsh[...] = dot(m.pt[...].astype(BF), m.ts[...].reshape(S, D)).astype(BF)

    def t2_range(lo, hi):
        @pl.loop(lo, hi)
        def _(i):
            c = pl.multiple_of(i * 512, 512)
            m.t2[:, pl.ds(c, 512)] = jnp.exp(dot(m.tsh[...], m.w_b[:, pl.ds(c, 512)]) * (1.0 / teacher_temp))

    t2_range(0, CL // 512)
    arrive(c_dq)
    c_dz = start([(m.dm.at[z], m.dm.at[z], dev) for dev in zdev])

    v2 = col_factor(1, c_cs)
    m.va[qd] = v2
    c_rs = send_rowsum(1)
    c_va = start([(m.va.at[qd], m.va.at[qd], dev) for dev in qdev])
    while steps:
        next_ring()

    @pl.loop(0, PAIRS)
    def _(k):
        tk = m.tq[pl.ds(k * 2, 2)].reshape(2 * T, D)
        for c in range(0, CZ, 512):
            e = jnp.exp(dot(tk, m.wz[:, c:c + 512]) * (1.0 / teacher_temp))
            hi = e.astype(BF)
            m.esp[k, 0:128, c:c + 512] = hi
            m.esp[k, 128:256, c:c + 512] = (e - hi.astype(F32)).astype(BF)

    def block_col(ref, k):
        rows = jnp.broadcast_to(ref[...].reshape(NR, 1, 128), (NR, RPR, 128)).reshape(512, 128)
        mine = (iota((NR, RPR, 128), 2) == iota((NR, RPR, 128), 1) + k * RPR).reshape(512, 128)
        return jnp.sum(jnp.where(mine, rows, 0.0), 1, keepdims=True)

    vbase = pl.multiple_of(lax.rem(z, Z // 4) * CZ, CZ) if Z >= 4 else None

    def v_layout1(c):
        if Z >= 4:
            return m.va[z // (Z // 4), :, pl.ds(pl.multiple_of(vbase + c, 256), 256)]
        per = 4 // Z
        q = z * per + c // CQ
        return m.va[q, :, pl.ds(pl.multiple_of(c % CQ, 256), 256)]

    def layout1(k):
        sk = m.stu[:, :, pl.ds(pl.multiple_of(k * RPR, RPR), RPR), :].reshape(512, D)
        m.st[k] = sk.T
        ic = block_col(m.meta, k)
        m.idxc[k] = jnp.broadcast_to(ic, (512, 128))
        sc = block_col(m.dm, k)
        hot = jnp.where(iota((512, 128), 1).astype(F32) == ic, 1.0, 0.0).astype(BF)
        hot = jnp.concatenate([hot, hot], 1)

        @pl.loop(0, CZ // 256)
        def _(i):
            c = pl.multiple_of(i * 256, 256)
            m.a1[k, :, pl.ds(c, 256)] = jnp.exp(dot(sk, m.wz[:, pl.ds(c, 256)]) * (1.0 / student_temp)) * sc
            m.t1[k, :, pl.ds(c, 256)] = dot(hot, m.esp[k, :, pl.ds(c, 256)]) * v_layout1(c)

    arrive(c_va)
    arrive(c_metaz)
    arrive(c_dz)
    arrive(ring[-1])
    for k in range(PAIRS // 2):
        layout1(k)
    u2 = row_factor(1, c_rs)
    m.ua[z] = u2 * (GS * TEACHERS)
    c_ua = start([(m.ua.at[z], m.ua.at[z], dev) for dev in zdev])
    for k in range(PAIRS // 2, PAIRS):
        layout1(k)
    arrive(c_ua)

    def quarter(z_, q):
        return m.ua[z_, :, q * T:(q + 1) * T]

    def own(z_):
        total = None
        for q in range(4):
            one = jnp.where(qd == q, quarter(z_, q), 0.0)
            total = one if total is None else total + one
        return total

    lane = iota((512, 128), 1).astype(F32)
    ucs = []
    for k in range(PAIRS):
        urow = jnp.concatenate([own(2 * k), own(2 * k + 1)], 1)
        ucs.append(jnp.sum(jnp.where(lane == m.idxc[k], jnp.broadcast_to(urow, (512, 128)), 0.0), 1, keepdims=True))

    def grad1(h):
        for c in range(h * CH, (h + 1) * CH, 256):
            total = None
            for k in range(PAIRS):
                g = (m.a1[k, :, c:c + 256] - m.t1[k, :, c:c + 256] * ucs[k]).astype(BF)
                one = dot(m.st[k], g)
                total = one if total is None else total + one
            at = c - h * CH
            m.ins[h, :, at:at + 256] = jnp.sum(m.wzf[:, c:c + 256] * total, 0, keepdims=True)
            for y_ in range(2):
                for z_ in range(Z):
                    for c_ in range(2):
                        f = ((y_ * Z + z_) * 2 + c_) * FB
                        m.gw[h, c_, y_, z_, :, at:at + 256] = total[f:f + FB, :]
        return (start([(m.gw.at[h, 1 - core], m.gwr.at[h], qdev[0])]),
                start([(m.ins.at[h], m.inr.at[h, d], dev) for d, dev in enumerate(qdev)]))

    c_gw, c_in, c_gy, c_gp = [None] * 2, [None] * 2, [None] * 2, [None] * 2
    c_gw[0], c_in[0] = grad1(0)

    def to_y(h):
        arrive(c_gw[h])
        m.gy[h] = m.gw[h, core, 1 - yl] + m.gwr[h, 1 - yl]
        c_gy[h] = start([(m.gy.at[h], m.gyr.at[h], qdev[1])])

    usort = []
    for q in range(4):
        for z_ in range(Z):
            usort.append(jnp.broadcast_to(quarter(z_, q), (B, T)))
    usort = jnp.concatenate(usort, 0)
    prow = m.msort[0][:, 0:64]
    for q in range(1, 4):
        prow = jnp.concatenate([prow, m.msort[q][:, 0:64]], 1)
    ztrow = jnp.broadcast_to(((iota((1, S), 1) >> (B.bit_length() - 1)) & 1).astype(F32) * T, (1, S))
    pcol = to_col(prow - ztrow, S)
    ucol = jnp.sum(jnp.where(iota((S, T), 1).astype(F32) == pcol, usort, 0.0), 1, keepdims=True)
    ucol = jnp.sum(m.pt[...] * to_row(ucol, S), 1, keepdims=True)

    def g2_step(i, acc):
        c = pl.multiple_of(i * 512, 512)
        q = (i * 512) // CQ
        w = min(512, CQ)
        if CQ >= 512:
            vv = m.va[q, :, pl.ds(pl.multiple_of(c - q * CQ, 512), 512)]
        else:
            vv = jnp.concatenate([m.va[q + j] for j in range(512 // CQ)], 1)
        g = (m.a2[:, pl.ds(c, 512)] * sc2 - m.t2[:, pl.ds(c, 512)] * vv * ucol).astype(BF)
        return acc + dotg(g, m.w_b[:, pl.ds(c, 512)], NT)

    gsum = lax.fori_loop(0, CL // 1024, g2_step, jnp.zeros((S, D), F32))
    to_y(0)
    gsum = lax.fori_loop(CL // 1024, CL // 512, g2_step, gsum)
    m.gu[...] = gsum.reshape(NP, RB, D)
    c_gu = start([(m.gu.at[p2], m.gur.at[d], dev) for d, (p2, dev) in enumerate(zip(ps, pdev))])
    c_gw[1], c_in[1] = grad1(1)

    def to_z(h):
        arrive(c_in[h])
        inner = m.ins[h] + m.inr[h, 0] + m.inr[h, 1] + m.inr[h, 2]
        arrive(c_gy[h])
        inv = 1.0 / m.nz[:, h * CH:(h + 1) * CH]
        for z_ in range(Z):
            f = pl.multiple_of(row(yl, z_, core) * FB, FB)
            mine = m.gw[h, core, yl, z_] + m.gwr[h, yl, z_] + m.gyr[h, z_]
            m.go[h, z_] = (mine - m.wzf[pl.ds(f, FB), h * CH:(h + 1) * CH] * inner) * inv
        m.gpr[h, z] = m.go[h, z]
        c_gp[h] = start([(m.go.at[h, z2], m.gpr.at[h, z], dev) for z2, dev in zip(zs, zdev)])

    to_y(1)
    to_z(0)

    arrive(c_gu)
    gsum = m.gu[p]
    for d in range(NP - 1):
        gsum = gsum + m.gur[d]
    su = stu_ref[pl.ds(pl.multiple_of(p * RB, RB), RB), :].astype(F32)
    un = jnp.sqrt(jnp.sum(su * su, 1, keepdims=True) + epsilon)
    su = su / un
    m.gsr[p] = (gsum - su * jnp.sum(su * gsum, 1, keepdims=True)) / un
    c_gs = start([(m.gsr.at[p], m.gsr.at[p], dev) for dev in pdev])

    to_z(1)
    for h in range(2):
        arrive(c_gp[h])
        for z_ in range(Z):
            c = z_ * CZ + h * CH
            gp_out[:, c:c + CH] = m.gpr[h, z_]
    arrive(c_gs)
    gs_out[...] = m.gsr[...].reshape(S, D)
    for h in sent:
        h.wait_send()


def body(teacher, students, prototypes, pairing, layout):
    NR = lax.axis_size("rows")
    NP = lax.axis_size("protos")
    T, D = teacher.shape
    S = students.shape[0]
    CL = prototypes.shape[1]
    dims = (NR, NP, T, S, D, CL)
    vmem = pl.BlockSpec(memory_space=pltpu.VMEM)
    scratch = [pltpu.VMEM(shape, dtype) for shape, dtype in plan(*dims).values()]
    scratch += [pltpu.SemaphoreType.DMA((NSEM,)), pltpu.SemaphoreType.DMA((NSEM,)), pltpu.SemaphoreType.DMA((5,))]
    return pl.pallas_call(
        functools.partial(kernel, dims),
        out_shape=(
            jax.ShapeDtypeStruct((S, D), F32),
            jax.ShapeDtypeStruct((D // NR, CL), F32),
        ),
        in_specs=[pl.BlockSpec(memory_space=pl.ANY)] * 5,
        out_specs=(vmem, vmem),
        scratch_shapes=scratch,
        compiler_params=pltpu.CompilerParams(
            collective_id=0, has_side_effects=True, vmem_limit_bytes=VMEM_MIB * 1024 * 1024
        ),
        name="distill",
    )(teacher, students, prototypes, layout.reshape(1, S), pairing.reshape(1, S))


def solution(mesh):
    in_specs = (P("rows", None), P("rows", None), P(None, "protos"), P("rows"), P("rows"))
    out_specs = (P("rows", None), P("rows", "protos"))
    return jax.shard_map(body, mesh=mesh, in_specs=in_specs, out_specs=out_specs, check_vma=False)
```

```python
import functools

import jax
import jax.numpy as jnp
from jax import lax
from jax.experimental import pallas as pl
from jax.experimental.pallas import tpu as pltpu
from jax.sharding import PartitionSpec as P

F32 = jnp.float32
BF = jnp.bfloat16
MESH = pl.DeviceIdType.MESH

epsilon = 1e-06
teacher_temp = 0.07
student_temp = 0.1
loss_scale = 16.0

NT = (((1,), (1,)), ((), ()))
TN = (((0,), (0,)), ((), ()))


def dot(a, b):
    return jnp.dot(a, b, preferred_element_type=F32)


def dotg(a, b, dims):
    return lax.dot_general(a, b, dims, preferred_element_type=F32)


def iota(shape, dim):
    return lax.broadcasted_iota(jnp.int32, shape, dim)


def to_col(row, n):
    eye = iota((n, n), 0) == iota((n, n), 1)
    return jnp.sum(jnp.where(eye, jnp.broadcast_to(row, (n, n)), 0.0), 1, keepdims=True)


def to_row(col, n):
    eye = iota((n, n), 0) == iota((n, n), 1)
    return jnp.sum(jnp.where(eye, jnp.broadcast_to(col, (n, n)), 0.0), 0, keepdims=True)


def lane_fold(x):
    total = x[:, 0:128]
    for k in range(1, x.shape[1] // 128):
        total = total + x[:, k * 128:(k + 1) * 128]
    return total


class Refs:
    pass


def plan(NR, NP, T, S, D, CL):
    Z = NR // 4
    CZ = CL // Z
    CQ = CL // 4
    FB = D // NR
    RB = S // NP
    PLANE = 4 * NP - 1
    shapes = dict(
        w_b=((D, CL), BF),
        tea=((T, D), BF),
        stu_in=((S, D), BF),
        row_of=((1, S), jnp.int32),
        tp=((4, T, D), BF),
        tq=((Z, T, D), BF),
        sb=((S, D), BF),
        pt=((S, S), F32),
        ssort=((4, S // 4, D), BF),
        msort=((4, 1, 128), F32),
        stu=((Z, 4, S // 4, D), BF),
        meta=((Z, 4, 1, 128), F32),
        wzf=((D, CZ), F32),
        wz=((D, CZ), BF),
        nz=((1, CZ), F32),
        a2=((S, CL), F32),
        t2=((S, CL), F32),
        dsrc=((1, S), F32),
        drecv=((NP - 1, 1, S), F32),
        dq=((4, 1, 128), F32),
        dm=((Z, 4, 1, 128), F32),
        e8=((4 * T, CQ), F32),
        esp=((Z // 2, 256, CZ), BF),
        cs=((2, 1, CQ), F32),
        csr=((2, Z - 1, 1, CQ), F32),
        rs=((2, 1, 4 * T), F32),
        rsr=((2, PLANE, 1, 4 * T), F32),
        ua=((Z, 1, 4 * T), F32),
        tss=((4, S // 4, D), BF),
        ts=((4, S // 4, D), BF),
        tsh=((S, D), BF),
        va=((4, 1, CQ), F32),
        a1=((Z // 2, 512, CZ), F32),
        t1=((Z // 2, 512, CZ), F32),
        st=((Z // 2, D, 512), BF),
        idxc=((Z // 2, 512, 128), F32),
        gu=((NP, RB, D), F32),
        gur=((NP - 1, RB, D), F32),
        gsr=((NP, RB, D), F32),
        gw=((2, 2, 2, Z, FB, CZ // 2), F32),
        gwr=((2, 2, Z, FB, CZ // 2), F32),
        gy=((2, Z, FB, CZ // 2), F32),
        gyr=((2, Z, FB, CZ // 2), F32),
        ins=((2, 1, CZ // 2), F32),
        inr=((2, 3, 1, CZ // 2), F32),
        go=((2, Z, FB, CZ // 2), F32),
        gpr=((2, Z, FB, CZ // 2), F32),
    )
    return shapes


NSEM = 224
VMEM_MIB = 52


def kernel(dims, tea_in, stu_in, proto_ref, row_in, gs_out, gp_out, *scratch):
    NR, NP, T, S, D, CL = dims
    Z = NR // 4
    CZ = CL // Z
    CQ = CL // 4
    CH = CZ // 2
    B = S // NR
    RPR = 2 * B
    FB = D // NR
    RB = S // NP
    PAIRS = Z // 2
    TEACHERS = T * NR
    PROTOS = CL * NP
    GS = loss_scale / student_temp
    names = list(plan(*dims))
    m = Refs()
    for name, ref in zip(names, scratch):
        setattr(m, name, ref)
    send_sem, recv_sem, local_sem = scratch[len(names):]
    tea_ref, stu_ref, row_ref = m.tea, m.stu_in, m.row_of

    load = pltpu.make_async_copy(proto_ref, m.w_b, local_sem.at[0])
    small = [
        pltpu.make_async_copy(src, dst, local_sem.at[1 + i])
        for i, (src, dst) in enumerate(((tea_in, tea_ref), (stu_in, stu_ref), (row_in, row_ref)))]
    for c in small:
        c.start()
    load.start()

    r = lax.axis_index("rows")
    p = lax.axis_index("protos")
    core = lax.rem(r, 2)
    z = lax.rem(r // 2, Z)
    yl = r // (2 * Z)
    qd = yl * 2 + core

    def row(y_, z_, c_):
        return (y_ * Z + z_) * 2 + c_

    zs = [lax.rem(z + d, Z) for d in range(1, Z)]
    zdev = [(row(yl, z2, core), p) for z2 in zs]
    ps = [lax.rem(p + d, NP) for d in range(1, NP)]
    pdev = [(r, p2) for p2 in ps]
    qs, qdev = [], []
    for d in (1, 2, 3):
        c2 = 1 - core if d & 1 else core
        y2 = 1 - yl if d & 2 else yl
        qs.append(y2 * 2 + c2)
        qdev.append((row(y2, z, c2), p))
    plane = pdev + qdev + [(r2, p2) for r2, _ in qdev for p2 in ps]

    sent = []
    counter = [0]

    def start(copies):
        handles = []
        for src, dst, dev in copies:
            i = counter[0]
            counter[0] += 1
            h = pltpu.make_async_remote_copy(
                src_ref=src, dst_ref=dst, send_sem=send_sem.at[i], recv_sem=recv_sem.at[i],
                device_id=dev, device_id_type=MESH)
            h.start()
            handles.append(h)
            sent.append(h)
        return handles

    def arrive(handles):
        for h in handles:
            h.wait_recv()

    bar = pltpu.get_barrier_semaphore()
    everyone = zdev + plane
    for dev in everyone:
        pl.semaphore_signal(bar, inc=1, device_id=dev, device_id_type=MESH)

    for c in small:
        c.wait()
    te = tea_ref[...].astype(F32)
    te = (te * (1.0 / jnp.sqrt(jnp.sum(te * te, 1, keepdims=True) + epsilon))).astype(BF)
    m.tp[qd] = te
    m.tq[z] = te
    pl.semaphore_wait(bar, len(everyone))
    c_tp = start([(m.tp.at[qd], m.tp.at[qd], dev) for dev in qdev])

    st = stu_ref[...].astype(F32)
    m.sb[...] = (st * (1.0 / jnp.sqrt(jnp.sum(st * st, 1, keepdims=True) + epsilon))).astype(BF)
    lay = row_ref[...] >> (T.bit_length() - 1)
    zt = (lay >> 1) & (Z - 1)
    key = (((lay >> (Z.bit_length())) * 2 + (lay & 1)) * Z + zt).astype(F32)
    kcol = to_col(key, S)
    same = (kcol == key) & (iota((S, S), 1) < iota((S, S), 0))
    pos = kcol * B + jnp.sum(jnp.where(same, 1.0, 0.0), 1, keepdims=True)
    m.pt[...] = jnp.where(iota((S, S), 1).astype(F32) == pos, 1.0, 0.0)
    idx = to_col(((zt & 1) * T + (row_ref[...] & (T - 1))).astype(F32), S)
    m.ssort[...] = dotg(m.pt[...].astype(BF), m.sb[...], TN).astype(BF).reshape(4, S // 4, D)
    isort = jnp.sum(m.pt[...] * idx, 0, keepdims=True)
    spare = jnp.zeros((1, 64), F32)
    for q in range(4):
        m.msort[q] = jnp.concatenate([isort[:, q * 64:(q + 1) * 64], spare], 1)
    m.stu[z, qd] = m.ssort[qd]
    m.meta[z, qd] = m.msort[qd]

    c_meta = start([(m.msort.at[q], m.meta.at[z, qd], dev) for q, dev in zip(qs, qdev)])
    c_stu = start([(m.ssort.at[q], m.stu.at[z, qd], dev) for q, dev in zip(qs, qdev)])

    load.wait()

    def unit(c):
        w = m.w_b[:, pl.ds(pl.multiple_of(c, 256), 256)].astype(F32)
        n = jnp.sqrt(jnp.sum(w * w, 0, keepdims=True) + epsilon)
        return w * (1.0 / n), n

    def unit_range(lo, hi):
        @pl.loop(lo, hi)
        def _(i):
            c = pl.multiple_of(i * 256, 256)
            m.w_b[:, pl.ds(c, 256)] = unit(c)[0].astype(BF)

    zbase = pl.multiple_of(z * CZ, CZ)

    @pl.loop(0, CZ // 256)
    def _(i):
        c = pl.multiple_of(i * 256, 256)
        w, n = unit(zbase + c)
        m.nz[:, pl.ds(c, 256)] = n
        m.wzf[:, pl.ds(c, 256)] = w
        m.wz[:, pl.ds(c, 256)] = w.astype(BF)

    base = pl.multiple_of(qd * CQ, CQ)
    unit_range(qd * (CQ // 256), (qd + 1) * (CQ // 256))

    arrive(c_tp)

    @pl.loop(0, CQ // 256)
    def _(i):
        c = pl.multiple_of(i * 256, 256)
        e = jnp.exp(dot(m.tp[...].reshape(4 * T, D), m.w_b[:, pl.ds(base + c, 256)]) * (1.0 / teacher_temp))
        m.e8[:, pl.ds(c, 256)] = e
        m.cs[0, :, pl.ds(c, 256)] = jnp.sum(e, 0, keepdims=True)

    c_cs = start([(m.cs.at[0], m.csr.at[0, d], dev) for d, dev in enumerate(zdev)])
    def col_factor(it, c_cs):
        arrive(c_cs)
        total = m.cs[it]
        for d in range(Z - 1):
            total = total + m.csr[it, d]
        return 1.0 / (PROTOS * total)

    def send_rowsum(it):
        acc = jnp.zeros((4 * T, 128), F32)
        for c in range(0, CQ, 256):
            acc = acc + lane_fold(m.e8[:, c:c + 256] * m.va[qd, :, c:c + 256])
        m.rs[it] = to_row(jnp.sum(acc, 1, keepdims=True), 4 * T)
        return start([(m.rs.at[it], m.rsr.at[it, d], dev) for d, dev in enumerate(plane)])

    def row_factor(it, c_rs):
        arrive(c_rs)
        total = m.rs[it]
        for d in range(len(plane)):
            total = total + m.rsr[it, d]
        return 1.0 / (TEACHERS * total)

    def send_piece(q):
        return start([(m.stu.at[z, q], m.stu.at[z, q], dev) for dev in zdev])

    c_tea = start([(m.tq.at[z], m.tq.at[z], dev) for dev in zdev])
    c_pieces = [send_piece(qd)]
    arrive(c_meta)
    arrive(c_stu)
    unit_range(0, qd * (CQ // 256))
    unit_range((qd + 1) * (CQ // 256), CL // 256)

    v1 = col_factor(0, c_cs)
    m.va[qd] = v1
    c_rs = send_rowsum(0)
    c_pieces.append(send_piece(qs[0]))
    c_pieces.append(send_piece(qs[1]))
    c_metaz = start([(m.meta.at[z], m.meta.at[z], dev) for dev in zdev])

    def a2_step(i, acc):
        c = pl.multiple_of(i * 512, 512)
        a = jnp.exp(dot(m.sb[...], m.w_b[:, pl.ds(c, 512)]) * (1.0 / student_temp))
        m.a2[:, pl.ds(c, 512)] = a
        return acc + lane_fold(a)

    acc = lax.fori_loop(0, CL // 512, a2_step, jnp.zeros((S, 128), F32))
    m.dsrc[...] = to_row(jnp.sum(acc, 1, keepdims=True), S)
    c_den = start([(m.dsrc, m.drecv.at[d], dev) for d, dev in enumerate(pdev)])

    u1 = row_factor(0, c_rs)
    uc1 = to_col(u1, 4 * T)
    for c in range(0, CQ, 256):
        m.cs[1, :, c:c + 256] = jnp.sum(m.e8[:, c:c + 256] * uc1, 0, keepdims=True)
    c_cs = start([(m.cs.at[1], m.csr.at[1, d], dev) for d, dev in enumerate(zdev)])
    c_pieces.append(send_piece(qs[2]))
    arrive(c_tea)

    for k in range(PAIRS):
        rows = jnp.broadcast_to(m.meta[z], (4, RPR, 128)).reshape(4 * RPR, 128)
        mine = iota((4, RPR, 128), 2) == iota((4, RPR, 128), 1) + k * RPR
        col = jnp.sum(jnp.where(mine.reshape(4 * RPR, 128), rows, 0.0), 1, keepdims=True)
        hot = jnp.where(iota((4 * RPR, 128), 1).astype(F32) == col, 1.0, 0.0).astype(BF)
        got = dot(hot, m.tq[2 * k:2 * k + 2].reshape(2 * T, D)).astype(BF)
        m.tss[:, k * RPR:(k + 1) * RPR, :] = got.reshape(4, RPR, D)
    m.ts[qd] = m.tss[qd]
    c_ts = start([(m.tss.at[q], m.ts.at[qd], dev) for q, dev in zip(qs, qdev)])

    arrive(c_den)
    den = m.dsrc[...]
    for d in range(NP - 1):
        den = den + m.drecv[d]
    sc2 = GS / to_col(den, S)
    scs = jnp.sum(m.pt[...] * sc2, 0, keepdims=True)
    for q in range(4):
        m.dq[q] = jnp.concatenate([scs[:, q * 64:(q + 1) * 64], spare], 1)
    m.dm[z, qd] = m.dq[qd]
    c_dq = start([(m.dq.at[q], m.dm.at[z, qd], dev) for q, dev in zip(qs, qdev)])

    @pl.loop(0, PAIRS)
    def _(k):
        tk = m.tq[pl.ds(k * 2, 2)].reshape(2 * T, D)
        for c in range(0, CZ, 512):
            e = jnp.exp(dot(tk, m.wz[:, c:c + 512]) * (1.0 / teacher_temp))
            hi = e.astype(BF)
            m.esp[k, 0:128, c:c + 512] = hi
            m.esp[k, 128:256, c:c + 512] = (e - hi.astype(F32)).astype(BF)

    arrive(c_dq)
    c_dz = start([(m.dm.at[z], m.dm.at[z], dev) for dev in zdev])

    v2 = col_factor(1, c_cs)
    m.va[qd] = v2
    c_rs = send_rowsum(1)
    c_va = start([(m.va.at[qd], m.va.at[qd], dev) for dev in qdev])
    arrive(c_ts)
    m.tsh[...] = dot(m.pt[...].astype(BF), m.ts[...].reshape(S, D)).astype(BF)

    def t2_range(lo, hi):
        @pl.loop(lo, hi)
        def _(i):
            c = pl.multiple_of(i * 512, 512)
            m.t2[:, pl.ds(c, 512)] = jnp.exp(dot(m.tsh[...], m.w_b[:, pl.ds(c, 512)]) * (1.0 / teacher_temp))

    t2_range(0, CL // 512)

    def block_col(ref, k):
        rows = jnp.broadcast_to(ref[...].reshape(NR, 1, 128), (NR, RPR, 128)).reshape(512, 128)
        mine = (iota((NR, RPR, 128), 2) == iota((NR, RPR, 128), 1) + k * RPR).reshape(512, 128)
        return jnp.sum(jnp.where(mine, rows, 0.0), 1, keepdims=True)

    vbase = pl.multiple_of(lax.rem(z, Z // 4) * CZ, CZ) if Z >= 4 else None

    def v_layout1(c):
        if Z >= 4:
            return m.va[z // (Z // 4), :, pl.ds(pl.multiple_of(vbase + c, 256), 256)]
        per = 4 // Z
        q = z * per + c // CQ
        return m.va[q, :, pl.ds(pl.multiple_of(c % CQ, 256), 256)]

    def layout1(k):
        sk = m.stu[:, :, pl.ds(pl.multiple_of(k * RPR, RPR), RPR), :].reshape(512, D)
        m.st[k] = sk.T
        ic = block_col(m.meta, k)
        m.idxc[k] = jnp.broadcast_to(ic, (512, 128))
        sc = block_col(m.dm, k)
        hot = jnp.where(iota((512, 128), 1).astype(F32) == ic, 1.0, 0.0).astype(BF)
        hot = jnp.concatenate([hot, hot], 1)

        @pl.loop(0, CZ // 256)
        def _(i):
            c = pl.multiple_of(i * 256, 256)
            m.a1[k, :, pl.ds(c, 256)] = jnp.exp(dot(sk, m.wz[:, pl.ds(c, 256)]) * (1.0 / student_temp)) * sc
            m.t1[k, :, pl.ds(c, 256)] = dot(hot, m.esp[k, :, pl.ds(c, 256)]) * v_layout1(c)

    arrive(c_va)
    arrive(c_metaz)
    arrive(c_dz)
    for c in c_pieces:
        arrive(c)
    for k in range(PAIRS // 4):
        layout1(k)
    u2 = row_factor(1, c_rs)
    m.ua[z] = u2 * (GS * TEACHERS)
    c_ua = start([(m.ua.at[z], m.ua.at[z], dev) for dev in zdev])
    for k in range(PAIRS // 4, PAIRS):
        layout1(k)
    arrive(c_ua)

    def quarter(z_, q):
        return m.ua[z_, :, q * T:(q + 1) * T]

    def own(z_):
        total = None
        for q in range(4):
            one = jnp.where(qd == q, quarter(z_, q), 0.0)
            total = one if total is None else total + one
        return total

    lane = iota((512, 128), 1).astype(F32)
    ucs = []
    for k in range(PAIRS):
        urow = jnp.concatenate([own(2 * k), own(2 * k + 1)], 1)
        ucs.append(jnp.sum(jnp.where(lane == m.idxc[k], jnp.broadcast_to(urow, (512, 128)), 0.0), 1, keepdims=True))

    def grad1(h):
        for c in range(h * CH, (h + 1) * CH, 256):
            total = None
            for k in range(PAIRS):
                g = (m.a1[k, :, c:c + 256] - m.t1[k, :, c:c + 256] * ucs[k]).astype(BF)
                one = dot(m.st[k], g)
                total = one if total is None else total + one
            at = c - h * CH
            m.ins[h, :, at:at + 256] = jnp.sum(m.wzf[:, c:c + 256] * total, 0, keepdims=True)
            for y_ in range(2):
                for z_ in range(Z):
                    for c_ in range(2):
                        f = ((y_ * Z + z_) * 2 + c_) * FB
                        m.gw[h, c_, y_, z_, :, at:at + 256] = total[f:f + FB, :]
        return (start([(m.gw.at[h, 1 - core], m.gwr.at[h], qdev[0])]),
                start([(m.ins.at[h], m.inr.at[h, d], dev) for d, dev in enumerate(qdev)]))

    c_gw, c_in, c_gy, c_gp = [None] * 2, [None] * 2, [None] * 2, [None] * 2
    c_gw[0], c_in[0] = grad1(0)

    def to_y(h):
        arrive(c_gw[h])
        m.gy[h] = m.gw[h, core, 1 - yl] + m.gwr[h, 1 - yl]
        c_gy[h] = start([(m.gy.at[h], m.gyr.at[h], qdev[1])])

    usort = []
    for q in range(4):
        for z_ in range(Z):
            usort.append(jnp.broadcast_to(quarter(z_, q), (B, T)))
    usort = jnp.concatenate(usort, 0)
    prow = m.msort[0][:, 0:64]
    for q in range(1, 4):
        prow = jnp.concatenate([prow, m.msort[q][:, 0:64]], 1)
    ztrow = jnp.broadcast_to(((iota((1, S), 1) >> (B.bit_length() - 1)) & 1).astype(F32) * T, (1, S))
    pcol = to_col(prow - ztrow, S)
    ucol = jnp.sum(jnp.where(iota((S, T), 1).astype(F32) == pcol, usort, 0.0), 1, keepdims=True)
    ucol = jnp.sum(m.pt[...] * to_row(ucol, S), 1, keepdims=True)

    def g2_step(i, acc):
        c = pl.multiple_of(i * 512, 512)
        q = (i * 512) // CQ
        w = min(512, CQ)
        if CQ >= 512:
            vv = m.va[q, :, pl.ds(pl.multiple_of(c - q * CQ, 512), 512)]
        else:
            vv = jnp.concatenate([m.va[q + j] for j in range(512 // CQ)], 1)
        g = (m.a2[:, pl.ds(c, 512)] * sc2 - m.t2[:, pl.ds(c, 512)] * vv * ucol).astype(BF)
        return acc + dotg(g, m.w_b[:, pl.ds(c, 512)], NT)

    gsum = lax.fori_loop(0, CL // 1024, g2_step, jnp.zeros((S, D), F32))
    to_y(0)
    gsum = lax.fori_loop(CL // 1024, CL // 512, g2_step, gsum)
    m.gu[...] = gsum.reshape(NP, RB, D)
    c_gu = start([(m.gu.at[p2], m.gur.at[d], dev) for d, (p2, dev) in enumerate(zip(ps, pdev))])
    c_gw[1], c_in[1] = grad1(1)

    def to_z(h):
        arrive(c_in[h])
        inner = m.ins[h] + m.inr[h, 0] + m.inr[h, 1] + m.inr[h, 2]
        arrive(c_gy[h])
        inv = 1.0 / m.nz[:, h * CH:(h + 1) * CH]
        for z_ in range(Z):
            f = pl.multiple_of(row(yl, z_, core) * FB, FB)
            mine = m.gw[h, core, yl, z_] + m.gwr[h, yl, z_] + m.gyr[h, z_]
            m.go[h, z_] = (mine - m.wzf[pl.ds(f, FB), h * CH:(h + 1) * CH] * inner) * inv
        m.gpr[h, z] = m.go[h, z]
        c_gp[h] = start([(m.go.at[h, z2], m.gpr.at[h, z], dev) for z2, dev in zip(zs, zdev)])

    to_y(1)
    to_z(0)

    arrive(c_gu)
    gsum = m.gu[p]
    for d in range(NP - 1):
        gsum = gsum + m.gur[d]
    su = stu_ref[pl.ds(pl.multiple_of(p * RB, RB), RB), :].astype(F32)
    un = jnp.sqrt(jnp.sum(su * su, 1, keepdims=True) + epsilon)
    su = su / un
    m.gsr[p] = (gsum - su * jnp.sum(su * gsum, 1, keepdims=True)) / un
    c_gs = start([(m.gsr.at[p], m.gsr.at[p], dev) for dev in pdev])

    to_z(1)
    for h in range(2):
        arrive(c_gp[h])
        for z_ in range(Z):
            c = z_ * CZ + h * CH
            gp_out[:, c:c + CH] = m.gpr[h, z_]
    arrive(c_gs)
    gs_out[...] = m.gsr[...].reshape(S, D)
    for h in sent:
        h.wait_send()


def body(teacher, students, prototypes, pairing, layout):
    NR = lax.axis_size("rows")
    NP = lax.axis_size("protos")
    T, D = teacher.shape
    S = students.shape[0]
    CL = prototypes.shape[1]
    dims = (NR, NP, T, S, D, CL)
    vmem = pl.BlockSpec(memory_space=pltpu.VMEM)
    scratch = [pltpu.VMEM(shape, dtype) for shape, dtype in plan(*dims).values()]
    scratch += [pltpu.SemaphoreType.DMA((NSEM,)), pltpu.SemaphoreType.DMA((NSEM,)), pltpu.SemaphoreType.DMA((5,))]
    return pl.pallas_call(
        functools.partial(kernel, dims),
        out_shape=(
            jax.ShapeDtypeStruct((S, D), F32),
            jax.ShapeDtypeStruct((D // NR, CL), F32),
        ),
        in_specs=[pl.BlockSpec(memory_space=pl.ANY)] * 4,
        out_specs=(vmem, vmem),
        scratch_shapes=scratch,
        compiler_params=pltpu.CompilerParams(
            collective_id=0, has_side_effects=True, vmem_limit_bytes=VMEM_MIB * 1024 * 1024
        ),
        name="distill",
    )(teacher, students, prototypes, (layout * T + pairing).reshape(1, S))


def solution(mesh):
    in_specs = (P("rows", None), P("rows", None), P(None, "protos"), P("rows"), P("rows"))
    out_specs = (P("rows", None), P("rows", "protos"))
    return jax.shard_map(body, mesh=mesh, in_specs=in_specs, out_specs=out_specs, check_vma=False)
```

```python
import functools

import jax
import jax.numpy as jnp
from jax import lax
from jax.experimental import pallas as pl
from jax.experimental.pallas import tpu as pltpu
from jax.sharding import PartitionSpec as P

F32 = jnp.float32
BF = jnp.bfloat16
MESH = pl.DeviceIdType.MESH

epsilon = 1e-06
teacher_temp = 0.07
student_temp = 0.1
loss_scale = 16.0

NT = (((1,), (1,)), ((), ()))
TN = (((0,), (0,)), ((), ()))


def dot(a, b):
    return jnp.dot(a, b, preferred_element_type=F32)


def dotg(a, b, dims):
    return lax.dot_general(a, b, dims, preferred_element_type=F32)


def iota(shape, dim):
    return lax.broadcasted_iota(jnp.int32, shape, dim)


def to_col(row, n):
    eye = iota((n, n), 0) == iota((n, n), 1)
    return jnp.sum(jnp.where(eye, jnp.broadcast_to(row, (n, n)), 0.0), 1, keepdims=True)


def to_row(col, n):
    eye = iota((n, n), 0) == iota((n, n), 1)
    return jnp.sum(jnp.where(eye, jnp.broadcast_to(col, (n, n)), 0.0), 0, keepdims=True)


def lane_fold(x):
    total = x[:, 0:128]
    for k in range(1, x.shape[1] // 128):
        total = total + x[:, k * 128:(k + 1) * 128]
    return total


class Refs:
    pass


def plan(NR, NP, T, S, D, CL):
    Z = NR // 4
    CZ = CL // Z
    CQ = CL // 4
    FB = D // NR
    RB = S // NP
    PLANE = 4 * NP - 1
    shapes = dict(
        w_b=((D, CL), BF),
        tea=((T, D), BF),
        stu_in=((S, D), BF),
        lay=((1, S), jnp.int32),
        pair=((1, S), jnp.int32),
        tp=((4, T, D), BF),
        tq=((Z, T, D), BF),
        sb=((S, D), BF),
        pt=((S, S), F32),
        ssort=((4, S // 4, D), BF),
        msort=((4, 1, 128), F32),
        stu=((Z, 4, S // 4, D), BF),
        meta=((Z, 4, 1, 128), F32),
        wzf=((D, CZ), F32),
        wz=((D, CZ), BF),
        nz=((1, CZ), F32),
        a2=((S, CL), F32),
        t2=((S, CL), F32),
        dsrc=((1, S), F32),
        drecv=((NP - 1, 1, S), F32),
        dq=((4, 1, 128), F32),
        dm=((Z, 4, 1, 128), F32),
        e8=((4 * T, CQ), F32),
        esp=((Z // 2, 256, CZ), BF),
        cs=((2, 1, CQ), F32),
        csr=((2, Z - 1, 1, CQ), F32),
        rs=((2, 1, 4 * T), F32),
        rsr=((2, PLANE, 1, 4 * T), F32),
        ua=((Z, 1, 4 * T), F32),
        tss=((4, S // 4, D), BF),
        ts=((4, S // 4, D), BF),
        tsh=((S, D), BF),
        va=((4, 1, CQ), F32),
        a1=((Z // 2, 512, CZ), F32),
        t1=((Z // 2, 512, CZ), F32),
        st=((Z // 2, D, 512), BF),
        idxc=((Z // 2, 512, 128), F32),
        gu=((NP, RB, D), F32),
        gur=((NP - 1, RB, D), F32),
        gsr=((NP, RB, D), F32),
        gw=((2, 2, 2, Z, FB, CZ // 2), F32),
        gwr=((2, 2, Z, FB, CZ // 2), F32),
        gy=((2, Z, FB, CZ // 2), F32),
        gyr=((2, Z, FB, CZ // 2), F32),
        ins=((2, 1, CZ // 2), F32),
        inr=((2, 3, 1, CZ // 2), F32),
        go=((2, Z, FB, CZ // 2), F32),
        gpr=((2, Z, FB, CZ // 2), F32),
    )
    return shapes


NSEM = 192
VMEM_MIB = 60


def kernel(dims, tea_in, stu_in, proto_ref, lay_in, pair_in, gs_out, gp_out, *scratch):
    NR, NP, T, S, D, CL = dims
    Z = NR // 4
    CZ = CL // Z
    CQ = CL // 4
    CH = CZ // 2
    B = S // NR
    RPR = 2 * B
    FB = D // NR
    RB = S // NP
    PAIRS = Z // 2
    TEACHERS = T * NR
    PROTOS = CL * NP
    GS = loss_scale / student_temp
    names = list(plan(*dims))
    m = Refs()
    for name, ref in zip(names, scratch):
        setattr(m, name, ref)
    send_sem, recv_sem, local_sem = scratch[len(names):]
    tea_ref, stu_ref, lay_ref, pair_ref = m.tea, m.stu_in, m.lay, m.pair

    load = pltpu.make_async_copy(proto_ref, m.w_b, local_sem.at[0])
    small = [
        pltpu.make_async_copy(src, dst, local_sem.at[1 + i])
        for i, (src, dst) in enumerate(((tea_in, tea_ref), (stu_in, stu_ref), (lay_in, lay_ref), (pair_in, pair_ref)))]
    for c in small:
        c.start()
    load.start()

    r = lax.axis_index("rows")
    p = lax.axis_index("protos")
    core = lax.rem(r, 2)
    z = lax.rem(r // 2, Z)
    yl = r // (2 * Z)
    qd = yl * 2 + core

    def row(y_, z_, c_):
        return (y_ * Z + z_) * 2 + c_

    zs = [lax.rem(z + d, Z) for d in range(1, Z)]
    zdev = [(row(yl, z2, core), p) for z2 in zs]
    ps = [lax.rem(p + d, NP) for d in range(1, NP)]
    pdev = [(r, p2) for p2 in ps]
    qs, qdev = [], []
    for d in (1, 2, 3):
        c2 = 1 - core if d & 1 else core
        y2 = 1 - yl if d & 2 else yl
        qs.append(y2 * 2 + c2)
        qdev.append((row(y2, z, c2), p))
    plane = pdev + qdev + [(r2, p2) for r2, _ in qdev for p2 in ps]

    sent = []
    counter = [0]

    def start(copies):
        handles = []
        for src, dst, dev in copies:
            i = counter[0]
            counter[0] += 1
            h = pltpu.make_async_remote_copy(
                src_ref=src, dst_ref=dst, send_sem=send_sem.at[i], recv_sem=recv_sem.at[i],
                device_id=dev, device_id_type=MESH)
            h.start()
            handles.append(h)
            sent.append(h)
        return handles

    def arrive(handles):
        for h in handles:
            h.wait_recv()

    bar = pltpu.get_barrier_semaphore()
    everyone = zdev + plane
    for dev in everyone:
        pl.semaphore_signal(bar, inc=1, device_id=dev, device_id_type=MESH)

    for c in small:
        c.wait()
    te = tea_ref[...].astype(F32)
    te = (te * (1.0 / jnp.sqrt(jnp.sum(te * te, 1, keepdims=True) + epsilon))).astype(BF)
    m.tp[qd] = te
    m.tq[z] = te
    pl.semaphore_wait(bar, len(everyone))
    c_tp = start([(m.tp.at[qd], m.tp.at[qd], dev) for dev in qdev])
    c_tea = start([(m.tq.at[z], m.tq.at[z], dev) for dev in zdev])

    st = stu_ref[...].astype(F32)
    m.sb[...] = (st * (1.0 / jnp.sqrt(jnp.sum(st * st, 1, keepdims=True) + epsilon))).astype(BF)
    lay = lay_ref[...]
    zt = (lay >> 1) & (Z - 1)
    key = (((lay >> (Z.bit_length())) * 2 + (lay & 1)) * Z + zt).astype(F32)
    kcol = to_col(key, S)
    same = (kcol == key) & (iota((S, S), 1) < iota((S, S), 0))
    pos = kcol * B + jnp.sum(jnp.where(same, 1.0, 0.0), 1, keepdims=True)
    m.pt[...] = jnp.where(iota((S, S), 1).astype(F32) == pos, 1.0, 0.0)
    idx = to_col(((zt & 1) * T + pair_ref[...]).astype(F32), S)
    m.ssort[...] = dotg(m.pt[...].astype(BF), m.sb[...], TN).astype(BF).reshape(4, S // 4, D)
    isort = jnp.sum(m.pt[...] * idx, 0, keepdims=True)
    spare = jnp.zeros((1, 64), F32)
    for q in range(4):
        m.msort[q] = jnp.concatenate([isort[:, q * 64:(q + 1) * 64], spare], 1)
    m.stu[z, qd] = m.ssort[qd]
    m.meta[z, qd] = m.msort[qd]

    c_meta = start([(m.msort.at[q], m.meta.at[z, qd], dev) for q, dev in zip(qs, qdev)])
    c_stu = start([(m.ssort.at[q], m.stu.at[z, qd], dev) for q, dev in zip(qs, qdev)])

    load.wait()

    def unit(c):
        w = m.w_b[:, pl.ds(pl.multiple_of(c, 256), 256)].astype(F32)
        n = jnp.sqrt(jnp.sum(w * w, 0, keepdims=True) + epsilon)
        return w * (1.0 / n), n

    def unit_range(lo, hi):
        @pl.loop(lo, hi)
        def _(i):
            c = pl.multiple_of(i * 256, 256)
            m.w_b[:, pl.ds(c, 256)] = unit(c)[0].astype(BF)

    zbase = pl.multiple_of(z * CZ, CZ)

    @pl.loop(0, CZ // 256)
    def _(i):
        c = pl.multiple_of(i * 256, 256)
        w, n = unit(zbase + c)
        m.nz[:, pl.ds(c, 256)] = n
        m.wzf[:, pl.ds(c, 256)] = w
        m.wz[:, pl.ds(c, 256)] = w.astype(BF)

    base = pl.multiple_of(qd * CQ, CQ)
    unit_range(qd * (CQ // 256), (qd + 1) * (CQ // 256))

    arrive(c_tp)

    @pl.loop(0, CQ // 256)
    def _(i):
        c = pl.multiple_of(i * 256, 256)
        e = jnp.exp(dot(m.tp[...].reshape(4 * T, D), m.w_b[:, pl.ds(base + c, 256)]) * (1.0 / teacher_temp))
        m.e8[:, pl.ds(c, 256)] = e
        m.cs[0, :, pl.ds(c, 256)] = jnp.sum(e, 0, keepdims=True)

    c_cs = start([(m.cs.at[0], m.csr.at[0, d], dev) for d, dev in enumerate(zdev)])
    def col_factor(it, c_cs):
        arrive(c_cs)
        total = m.cs[it]
        for d in range(Z - 1):
            total = total + m.csr[it, d]
        return 1.0 / (PROTOS * total)

    def send_rowsum(it):
        acc = jnp.zeros((4 * T, 128), F32)
        for c in range(0, CQ, 256):
            acc = acc + lane_fold(m.e8[:, c:c + 256] * m.va[qd, :, c:c + 256])
        m.rs[it] = to_row(jnp.sum(acc, 1, keepdims=True), 4 * T)
        return start([(m.rs.at[it], m.rsr.at[it, d], dev) for d, dev in enumerate(plane)])

    def row_factor(it, c_rs):
        arrive(c_rs)
        total = m.rs[it]
        for d in range(len(plane)):
            total = total + m.rsr[it, d]
        return 1.0 / (TEACHERS * total)

    zr, zl = lax.rem(z + 1, Z), lax.rem(z + Z - 1, Z)
    right, left = (row(yl, zr, core), p), (row(yl, zl, core), p)
    ring = []

    def ring_step(s):
        if ring:
            arrive(ring[-1])
        a = lax.rem(z + Z - (s - 1), Z)
        b = lax.rem(z + (s - 1), Z)
        if s < Z // 2:
            ring.append(start([(m.stu.at[a], m.stu.at[a], right), (m.stu.at[b], m.stu.at[b], left)]))
        else:
            ring.append(start([
                (m.stu.at[a, pl.ds(0, 2)], m.stu.at[a, pl.ds(0, 2)], right),
                (m.stu.at[b, pl.ds(2, 2)], m.stu.at[b, pl.ds(2, 2)], left)]))

    steps = list(range(1, Z // 2 + 1))

    def next_ring():
        if steps:
            ring_step(steps.pop(0))

    arrive(c_meta)
    arrive(c_stu)
    next_ring()
    unit_range(0, qd * (CQ // 256))
    unit_range((qd + 1) * (CQ // 256), CL // 256)

    v1 = col_factor(0, c_cs)
    m.va[qd] = v1
    c_rs = send_rowsum(0)
    next_ring()
    c_metaz = start([(m.meta.at[z], m.meta.at[z], dev) for dev in zdev])

    def a2_step(i, acc):
        c = pl.multiple_of(i * 512, 512)
        a = jnp.exp(dot(m.sb[...], m.w_b[:, pl.ds(c, 512)]) * (1.0 / student_temp))
        m.a2[:, pl.ds(c, 512)] = a
        return acc + lane_fold(a)

    acc = lax.fori_loop(0, CL // 512, a2_step, jnp.zeros((S, 128), F32))
    m.dsrc[...] = to_row(jnp.sum(acc, 1, keepdims=True), S)
    c_den = start([(m.dsrc, m.drecv.at[d], dev) for d, dev in enumerate(pdev)])
    arrive(c_tea)

    for k in range(PAIRS):
        rows = jnp.broadcast_to(m.meta[z], (4, RPR, 128)).reshape(4 * RPR, 128)
        mine = iota((4, RPR, 128), 2) == iota((4, RPR, 128), 1) + k * RPR
        col = jnp.sum(jnp.where(mine.reshape(4 * RPR, 128), rows, 0.0), 1, keepdims=True)
        hot = jnp.where(iota((4 * RPR, 128), 1).astype(F32) == col, 1.0, 0.0).astype(BF)
        got = dot(hot, m.tq[2 * k:2 * k + 2].reshape(2 * T, D)).astype(BF)
        m.tss[:, k * RPR:(k + 1) * RPR, :] = got.reshape(4, RPR, D)
    m.ts[qd] = m.tss[qd]
    c_ts = start([(m.tss.at[q], m.ts.at[qd], dev) for q, dev in zip(qs, qdev)])

    u1 = row_factor(0, c_rs)
    uc1 = to_col(u1, 4 * T)
    for c in range(0, CQ, 256):
        m.cs[1, :, c:c + 256] = jnp.sum(m.e8[:, c:c + 256] * uc1, 0, keepdims=True)
    c_cs = start([(m.cs.at[1], m.csr.at[1, d], dev) for d, dev in enumerate(zdev)])

    arrive(c_den)
    den = m.dsrc[...]
    for d in range(NP - 1):
        den = den + m.drecv[d]
    sc2 = GS / to_col(den, S)
    scs = jnp.sum(m.pt[...] * sc2, 0, keepdims=True)
    for q in range(4):
        m.dq[q] = jnp.concatenate([scs[:, q * 64:(q + 1) * 64], spare], 1)
    m.dm[z, qd] = m.dq[qd]
    c_dq = start([(m.dq.at[q], m.dm.at[z, qd], dev) for q, dev in zip(qs, qdev)])

    next_ring()
    arrive(c_ts)
    m.tsh[...] = dot(m.pt[...].astype(BF), m.ts[...].reshape(S, D)).astype(BF)

    def t2_range(lo, hi):
        @pl.loop(lo, hi)
        def _(i):
            c = pl.multiple_of(i * 512, 512)
            m.t2[:, pl.ds(c, 512)] = jnp.exp(dot(m.tsh[...], m.w_b[:, pl.ds(c, 512)]) * (1.0 / teacher_temp))

    t2_range(0, CL // 512)
    arrive(c_dq)
    c_dz = start([(m.dm.at[z], m.dm.at[z], dev) for dev in zdev])

    v2 = col_factor(1, c_cs)
    m.va[qd] = v2
    c_rs = send_rowsum(1)
    c_va = start([(m.va.at[qd], m.va.at[qd], dev) for dev in qdev])
    while steps:
        next_ring()

    @pl.loop(0, PAIRS)
    def _(k):
        tk = m.tq[pl.ds(k * 2, 2)].reshape(2 * T, D)
        for c in range(0, CZ, 512):
            e = jnp.exp(dot(tk, m.wz[:, c:c + 512]) * (1.0 / teacher_temp))
            hi = e.astype(BF)
            m.esp[k, 0:128, c:c + 512] = hi
            m.esp[k, 128:256, c:c + 512] = (e - hi.astype(F32)).astype(BF)

    def block_col(ref, k):
        rows = jnp.broadcast_to(ref[...].reshape(NR, 1, 128), (NR, RPR, 128)).reshape(512, 128)
        mine = (iota((NR, RPR, 128), 2) == iota((NR, RPR, 128), 1) + k * RPR).reshape(512, 128)
        return jnp.sum(jnp.where(mine, rows, 0.0), 1, keepdims=True)

    vbase = pl.multiple_of(lax.rem(z, Z // 4) * CZ, CZ) if Z >= 4 else None

    def v_layout1(c):
        if Z >= 4:
            return m.va[z // (Z // 4), :, pl.ds(pl.multiple_of(vbase + c, 256), 256)]
        per = 4 // Z
        q = z * per + c // CQ
        return m.va[q, :, pl.ds(pl.multiple_of(c % CQ, 256), 256)]

    def layout1(k):
        sk = m.stu[:, :, pl.ds(pl.multiple_of(k * RPR, RPR), RPR), :].reshape(512, D)
        m.st[k] = sk.T
        ic = block_col(m.meta, k)
        m.idxc[k] = jnp.broadcast_to(ic, (512, 128))
        sc = block_col(m.dm, k)
        hot = jnp.where(iota((512, 128), 1).astype(F32) == ic, 1.0, 0.0).astype(BF)
        hot = jnp.concatenate([hot, hot], 1)

        @pl.loop(0, CZ // 256)
        def _(i):
            c = pl.multiple_of(i * 256, 256)
            m.a1[k, :, pl.ds(c, 256)] = jnp.exp(dot(sk, m.wz[:, pl.ds(c, 256)]) * (1.0 / student_temp)) * sc
            m.t1[k, :, pl.ds(c, 256)] = dot(hot, m.esp[k, :, pl.ds(c, 256)]) * v_layout1(c)

    arrive(c_va)
    arrive(c_metaz)
    arrive(c_dz)
    arrive(ring[-1])
    for k in range(PAIRS // 2):
        layout1(k)
    u2 = row_factor(1, c_rs)
    m.ua[z] = u2 * (GS * TEACHERS)
    c_ua = start([(m.ua.at[z], m.ua.at[z], dev) for dev in zdev])
    for k in range(PAIRS // 2, PAIRS):
        layout1(k)
    arrive(c_ua)

    def quarter(z_, q):
        return m.ua[z_, :, q * T:(q + 1) * T]

    def own(z_):
        total = None
        for q in range(4):
            one = jnp.where(qd == q, quarter(z_, q), 0.0)
            total = one if total is None else total + one
        return total

    lane = iota((512, 128), 1).astype(F32)
    ucs = []
    for k in range(PAIRS):
        urow = jnp.concatenate([own(2 * k), own(2 * k + 1)], 1)
        ucs.append(jnp.sum(jnp.where(lane == m.idxc[k], jnp.broadcast_to(urow, (512, 128)), 0.0), 1, keepdims=True))

    def grad1(h):
        for c in range(h * CH, (h + 1) * CH, 256):
            total = None
            for k in range(PAIRS):
                g = (m.a1[k, :, c:c + 256] - m.t1[k, :, c:c + 256] * ucs[k]).astype(BF)
                one = dot(m.st[k], g)
                total = one if total is None else total + one
            at = c - h * CH
            m.ins[h, :, at:at + 256] = jnp.sum(m.wzf[:, c:c + 256] * total, 0, keepdims=True)
            for y_ in range(2):
                for z_ in range(Z):
                    for c_ in range(2):
                        f = ((y_ * Z + z_) * 2 + c_) * FB
                        m.gw[h, c_, y_, z_, :, at:at + 256] = total[f:f + FB, :]
        return (start([(m.gw.at[h, 1 - core], m.gwr.at[h], qdev[0])]),
                start([(m.ins.at[h], m.inr.at[h, d], dev) for d, dev in enumerate(qdev)]))

    c_gw, c_in, c_gy, c_gp = [None] * 2, [None] * 2, [None] * 2, [None] * 2
    c_gw[0], c_in[0] = grad1(0)

    def to_y(h):
        arrive(c_gw[h])
        m.gy[h] = m.gw[h, core, 1 - yl] + m.gwr[h, 1 - yl]
        c_gy[h] = start([(m.gy.at[h], m.gyr.at[h], qdev[1])])

    usort = []
    for q in range(4):
        for z_ in range(Z):
            usort.append(jnp.broadcast_to(quarter(z_, q), (B, T)))
    usort = jnp.concatenate(usort, 0)
    prow = m.msort[0][:, 0:64]
    for q in range(1, 4):
        prow = jnp.concatenate([prow, m.msort[q][:, 0:64]], 1)
    ztrow = jnp.broadcast_to(((iota((1, S), 1) >> (B.bit_length() - 1)) & 1).astype(F32) * T, (1, S))
    pcol = to_col(prow - ztrow, S)
    ucol = jnp.sum(jnp.where(iota((S, T), 1).astype(F32) == pcol, usort, 0.0), 1, keepdims=True)
    ucol = jnp.sum(m.pt[...] * to_row(ucol, S), 1, keepdims=True)

    def g2_step(i, acc):
        c = pl.multiple_of(i * 512, 512)
        q = (i * 512) // CQ
        w = min(512, CQ)
        if CQ >= 512:
            vv = m.va[q, :, pl.ds(pl.multiple_of(c - q * CQ, 512), 512)]
        else:
            vv = jnp.concatenate([m.va[q + j] for j in range(512 // CQ)], 1)
        g = (m.a2[:, pl.ds(c, 512)] * sc2 - m.t2[:, pl.ds(c, 512)] * vv * ucol).astype(BF)
        return acc + dotg(g, m.w_b[:, pl.ds(c, 512)], NT)

    gsum = lax.fori_loop(0, CL // 1024, g2_step, jnp.zeros((S, D), F32))
    to_y(0)
    gsum = lax.fori_loop(CL // 1024, CL // 512, g2_step, gsum)
    m.gu[...] = gsum.reshape(NP, RB, D)
    c_gu = start([(m.gu.at[p2], m.gur.at[d], dev) for d, (p2, dev) in enumerate(zip(ps, pdev))])
    c_gw[1], c_in[1] = grad1(1)

    def to_z(h):
        arrive(c_in[h])
        inner = m.ins[h] + m.inr[h, 0] + m.inr[h, 1] + m.inr[h, 2]
        arrive(c_gy[h])
        inv = 1.0 / m.nz[:, h * CH:(h + 1) * CH]
        for z_ in range(Z):
            f = pl.multiple_of(row(yl, z_, core) * FB, FB)
            mine = m.gw[h, core, yl, z_] + m.gwr[h, yl, z_] + m.gyr[h, z_]
            m.go[h, z_] = (mine - m.wzf[pl.ds(f, FB), h * CH:(h + 1) * CH] * inner) * inv
        m.gpr[h, z] = m.go[h, z]
        c_gp[h] = start([(m.go.at[h, z2], m.gpr.at[h, z], dev) for z2, dev in zip(zs, zdev)])

    to_y(1)
    to_z(0)

    arrive(c_gu)
    gsum = m.gu[p]
    for d in range(NP - 1):
        gsum = gsum + m.gur[d]
    su = stu_ref[pl.ds(pl.multiple_of(p * RB, RB), RB), :].astype(F32)
    un = jnp.sqrt(jnp.sum(su * su, 1, keepdims=True) + epsilon)
    su = su / un
    m.gsr[p] = (gsum - su * jnp.sum(su * gsum, 1, keepdims=True)) / un
    c_gs = start([(m.gsr.at[p], m.gsr.at[p], dev) for dev in pdev])

    to_z(1)
    for h in range(2):
        arrive(c_gp[h])
        for z_ in range(Z):
            c = z_ * CZ + h * CH
            gp_out[:, c:c + CH] = m.gpr[h, z_]
    arrive(c_gs)
    gs_out[...] = m.gsr[...].reshape(S, D)
    for h in sent:
        h.wait_send()


def body(teacher, students, prototypes, pairing, layout):
    NR = lax.axis_size("rows")
    NP = lax.axis_size("protos")
    T, D = teacher.shape
    S = students.shape[0]
    CL = prototypes.shape[1]
    dims = (NR, NP, T, S, D, CL)
    vmem = pl.BlockSpec(memory_space=pltpu.VMEM)
    scratch = [pltpu.VMEM(shape, dtype) for shape, dtype in plan(*dims).values()]
    scratch += [pltpu.SemaphoreType.DMA((NSEM,)), pltpu.SemaphoreType.DMA((NSEM,)), pltpu.SemaphoreType.DMA((5,))]
    return pl.pallas_call(
        functools.partial(kernel, dims),
        out_shape=(
            jax.ShapeDtypeStruct((S, D), F32),
            jax.ShapeDtypeStruct((D // NR, CL), F32),
        ),
        in_specs=[pl.BlockSpec(memory_space=pl.ANY)] * 5,
        out_specs=(vmem, vmem),
        scratch_shapes=scratch,
        compiler_params=pltpu.CompilerParams(
            collective_id=0, has_side_effects=True, vmem_limit_bytes=VMEM_MIB * 1024 * 1024
        ),
        name="distill",
    )(teacher, students, prototypes, layout.reshape(1, S), pairing.reshape(1, S))


def solution(mesh):
    in_specs = (P("rows", None), P("rows", None), P(None, "protos"), P("rows"), P("rows"))
    out_specs = (P("rows", None), P("rows", "protos"))
    return jax.shard_map(body, mesh=mesh, in_specs=in_specs, out_specs=out_specs, check_vma=False)
```

```python
import functools

import jax
import jax.numpy as jnp
from jax import lax
from jax.experimental import pallas as pl
from jax.experimental.pallas import tpu as pltpu
from jax.sharding import PartitionSpec as P

F32 = jnp.float32
BF = jnp.bfloat16
MESH = pl.DeviceIdType.MESH

epsilon = 1e-06
teacher_temp = 0.07
student_temp = 0.1
loss_scale = 16.0

NT = (((1,), (1,)), ((), ()))
TN = (((0,), (0,)), ((), ()))


def dot(a, b):
    return jnp.dot(a, b, preferred_element_type=F32)


def dotg(a, b, dims):
    return lax.dot_general(a, b, dims, preferred_element_type=F32)


def iota(shape, dim):
    return lax.broadcasted_iota(jnp.int32, shape, dim)


def to_col(row, n):
    eye = iota((n, n), 0) == iota((n, n), 1)
    return jnp.sum(jnp.where(eye, jnp.broadcast_to(row, (n, n)), 0.0), 1, keepdims=True)


def to_row(col, n):
    eye = iota((n, n), 0) == iota((n, n), 1)
    return jnp.sum(jnp.where(eye, jnp.broadcast_to(col, (n, n)), 0.0), 0, keepdims=True)


def lane_fold(x):
    total = x[:, 0:128]
    for k in range(1, x.shape[1] // 128):
        total = total + x[:, k * 128:(k + 1) * 128]
    return total


class Refs:
    pass


def plan(NR, NP, T, S, D, CL):
    Z = NR // 4
    CZ = CL // Z
    CQ = CL // 4
    FB = D // NR
    RB = S // NP
    PLANE = 4 * NP - 1
    shapes = dict(
        w_b=((D, CL), BF),
        tea=((T, D), BF),
        stu_in=((S, D), BF),
        lay=((1, S), jnp.int32),
        pair=((1, S), jnp.int32),
        tp=((4, T, D), BF),
        tq=((Z, T, D), BF),
        sb=((S, D), BF),
        pt=((S, S), F32),
        ssort=((4, S // 4, D), BF),
        msort=((4, 1, 128), F32),
        stu=((Z, 4, S // 4, D), BF),
        meta=((Z, 4, 1, 128), F32),
        wzf=((D, CZ), F32),
        wz=((D, CZ), BF),
        nz=((1, CZ), F32),
        a2=((S, CL), F32),
        t2=((S, CL), F32),
        dsrc=((1, S), F32),
        drecv=((NP - 1, 1, S), F32),
        dq=((4, 1, 128), F32),
        dm=((Z, 4, 1, 128), F32),
        e8=((4 * T, CQ), F32),
        esp=((Z // 2, 256, CZ), BF),
        cs=((2, 1, CQ), F32),
        csr=((2, Z - 1, 1, CQ), F32),
        rs=((2, 1, 4 * T), F32),
        rsr=((2, PLANE, 1, 4 * T), F32),
        ua=((Z, 1, 4 * T), F32),
        tss=((4, S // 4, D), BF),
        ts=((4, S // 4, D), BF),
        tsh=((S, D), BF),
        va=((4, 1, CQ), F32),
        a1=((Z // 2, 512, CZ), F32),
        t1=((Z // 2, 512, CZ), F32),
        st=((Z // 2, D, 512), BF),
        idxc=((Z // 2, 512, 128), F32),
        gu=((NP, RB, D), F32),
        gur=((NP - 1, RB, D), F32),
        gsr=((NP, RB, D), F32),
        gw=((2, 2, 2, Z, FB, CZ // 2), F32),
        gwr=((2, 2, Z, FB, CZ // 2), F32),
        gy=((2, Z, FB, CZ // 2), F32),
        gyr=((2, Z, FB, CZ // 2), F32),
        ins=((2, 1, CZ // 2), F32),
        inr=((2, 3, 1, CZ // 2), F32),
        go=((2, Z, FB, CZ // 2), F32),
        gpr=((2, Z, FB, CZ // 2), F32),
    )
    return shapes


NSEM = 192
VMEM_MIB = 60


def kernel(dims, tea_in, stu_in, proto_ref, lay_in, pair_in, gs_out, gp_out, *scratch):
    NR, NP, T, S, D, CL = dims
    Z = NR // 4
    CZ = CL // Z
    CQ = CL // 4
    CH = CZ // 2
    B = S // NR
    RPR = 2 * B
    FB = D // NR
    RB = S // NP
    PAIRS = Z // 2
    TEACHERS = T * NR
    PROTOS = CL * NP
    GS = loss_scale / student_temp
    names = list(plan(*dims))
    m = Refs()
    for name, ref in zip(names, scratch):
        setattr(m, name, ref)
    send_sem, recv_sem, local_sem = scratch[len(names):]
    tea_ref, stu_ref, lay_ref, pair_ref = m.tea, m.stu_in, m.lay, m.pair

    load = pltpu.make_async_copy(proto_ref, m.w_b, local_sem.at[0])
    small = [
        pltpu.make_async_copy(src, dst, local_sem.at[1 + i])
        for i, (src, dst) in enumerate(((tea_in, tea_ref), (stu_in, stu_ref), (lay_in, lay_ref), (pair_in, pair_ref)))]
    for c in small:
        c.start()
    load.start()

    r = lax.axis_index("rows")
    p = lax.axis_index("protos")
    core = lax.rem(r, 2)
    z = lax.rem(r // 2, Z)
    yl = r // (2 * Z)
    qd = yl * 2 + core

    def row(y_, z_, c_):
        return (y_ * Z + z_) * 2 + c_

    zs = [lax.rem(z + d, Z) for d in range(1, Z)]
    zdev = [(row(yl, z2, core), p) for z2 in zs]
    ps = [lax.rem(p + d, NP) for d in range(1, NP)]
    pdev = [(r, p2) for p2 in ps]
    qs, qdev = [], []
    for d in (1, 2, 3):
        c2 = 1 - core if d & 1 else core
        y2 = 1 - yl if d & 2 else yl
        qs.append(y2 * 2 + c2)
        qdev.append((row(y2, z, c2), p))
    plane = pdev + qdev + [(r2, p2) for r2, _ in qdev for p2 in ps]

    sent = []
    counter = [0]

    def start(copies):
        handles = []
        for src, dst, dev in copies:
            i = counter[0]
            counter[0] += 1
            h = pltpu.make_async_remote_copy(
                src_ref=src, dst_ref=dst, send_sem=send_sem.at[i], recv_sem=recv_sem.at[i],
                device_id=dev, device_id_type=MESH)
            h.start()
            handles.append(h)
            sent.append(h)
        return handles

    def arrive(handles):
        for h in handles:
            h.wait_recv()

    bar = pltpu.get_barrier_semaphore()
    everyone = zdev + plane
    for dev in everyone:
        pl.semaphore_signal(bar, inc=1, device_id=dev, device_id_type=MESH)

    for c in small:
        c.wait()
    te = tea_ref[...].astype(F32)
    te = (te * (1.0 / jnp.sqrt(jnp.sum(te * te, 1, keepdims=True) + epsilon))).astype(BF)
    m.tp[qd] = te
    m.tq[z] = te
    pl.semaphore_wait(bar, len(everyone))
    c_tp = start([(m.tp.at[qd], m.tp.at[qd], dev) for dev in qdev])
    c_tea = start([(m.tq.at[z], m.tq.at[z], dev) for dev in zdev])

    st = stu_ref[...].astype(F32)
    m.sb[...] = (st * (1.0 / jnp.sqrt(jnp.sum(st * st, 1, keepdims=True) + epsilon))).astype(BF)
    lay = lay_ref[...]
    zt = (lay >> 1) & (Z - 1)
    key = (((lay >> (Z.bit_length())) * 2 + (lay & 1)) * Z + zt).astype(F32)
    kcol = to_col(key, S)
    same = (kcol == key) & (iota((S, S), 1) < iota((S, S), 0))
    pos = kcol * B + jnp.sum(jnp.where(same, 1.0, 0.0), 1, keepdims=True)
    m.pt[...] = jnp.where(iota((S, S), 1).astype(F32) == pos, 1.0, 0.0)
    idx = to_col(((zt & 1) * T + pair_ref[...]).astype(F32), S)
    m.ssort[...] = dotg(m.pt[...].astype(BF), m.sb[...], TN).astype(BF).reshape(4, S // 4, D)
    isort = jnp.sum(m.pt[...] * idx, 0, keepdims=True)
    spare = jnp.zeros((1, 64), F32)
    for q in range(4):
        m.msort[q] = jnp.concatenate([isort[:, q * 64:(q + 1) * 64], spare], 1)
    m.stu[z, qd] = m.ssort[qd]
    m.meta[z, qd] = m.msort[qd]

    c_meta = start([(m.msort.at[q], m.meta.at[z, qd], dev) for q, dev in zip(qs, qdev)])
    c_stu = start([(m.ssort.at[q], m.stu.at[z, qd], dev) for q, dev in zip(qs, qdev)])

    load.wait()

    def unit(c):
        w = m.w_b[:, pl.ds(pl.multiple_of(c, 256), 256)].astype(F32)
        n = jnp.sqrt(jnp.sum(w * w, 0, keepdims=True) + epsilon)
        return w * (1.0 / n), n

    def unit_range(lo, hi):
        @pl.loop(lo, hi)
        def _(i):
            c = pl.multiple_of(i * 256, 256)
            m.w_b[:, pl.ds(c, 256)] = unit(c)[0].astype(BF)

    zbase = pl.multiple_of(z * CZ, CZ)

    @pl.loop(0, CZ // 256)
    def _(i):
        c = pl.multiple_of(i * 256, 256)
        w, n = unit(zbase + c)
        m.nz[:, pl.ds(c, 256)] = n
        m.wzf[:, pl.ds(c, 256)] = w
        m.wz[:, pl.ds(c, 256)] = w.astype(BF)

    base = pl.multiple_of(qd * CQ, CQ)
    unit_range(qd * (CQ // 256), (qd + 1) * (CQ // 256))

    arrive(c_tp)

    @pl.loop(0, CQ // 256)
    def _(i):
        c = pl.multiple_of(i * 256, 256)
        e = jnp.exp(dot(m.tp[...].reshape(4 * T, D), m.w_b[:, pl.ds(base + c, 256)]) * (1.0 / teacher_temp))
        m.e8[:, pl.ds(c, 256)] = e
        m.cs[0, :, pl.ds(c, 256)] = jnp.sum(e, 0, keepdims=True)

    c_cs = start([(m.cs.at[0], m.csr.at[0, d], dev) for d, dev in enumerate(zdev)])
    def col_factor(it, c_cs):
        arrive(c_cs)
        total = m.cs[it]
        for d in range(Z - 1):
            total = total + m.csr[it, d]
        return 1.0 / (PROTOS * total)

    def send_rowsum(it):
        acc = jnp.zeros((4 * T, 128), F32)
        for c in range(0, CQ, 256):
            acc = acc + lane_fold(m.e8[:, c:c + 256] * m.va[qd, :, c:c + 256])
        m.rs[it] = to_row(jnp.sum(acc, 1, keepdims=True), 4 * T)
        return start([(m.rs.at[it], m.rsr.at[it, d], dev) for d, dev in enumerate(plane)])

    def row_factor(it, c_rs):
        arrive(c_rs)
        total = m.rs[it]
        for d in range(len(plane)):
            total = total + m.rsr[it, d]
        return 1.0 / (TEACHERS * total)

    zr, zl = lax.rem(z + 1, Z), lax.rem(z + Z - 1, Z)
    right, left = (row(yl, zr, core), p), (row(yl, zl, core), p)
    ring = []

    def ring_step(s):
        if ring:
            arrive(ring[-1])
        a = lax.rem(z + Z - (s - 1), Z)
        b = lax.rem(z + (s - 1), Z)
        if s < Z // 2:
            ring.append(start([(m.stu.at[a], m.stu.at[a], right), (m.stu.at[b], m.stu.at[b], left)]))
        else:
            ring.append(start([
                (m.stu.at[a, pl.ds(0, 2)], m.stu.at[a, pl.ds(0, 2)], right),
                (m.stu.at[b, pl.ds(2, 2)], m.stu.at[b, pl.ds(2, 2)], left)]))

    steps = list(range(1, Z // 2 + 1))

    def next_ring():
        if steps:
            ring_step(steps.pop(0))

    arrive(c_meta)
    arrive(c_stu)
    next_ring()
    unit_range(0, qd * (CQ // 256))
    unit_range((qd + 1) * (CQ // 256), CL // 256)

    v1 = col_factor(0, c_cs)
    m.va[qd] = v1
    c_rs = send_rowsum(0)
    next_ring()
    c_metaz = start([(m.meta.at[z], m.meta.at[z], dev) for dev in zdev])

    def a2_step(i, acc):
        c = pl.multiple_of(i * 512, 512)
        a = jnp.exp(dot(m.sb[...], m.w_b[:, pl.ds(c, 512)]) * (1.0 / student_temp))
        m.a2[:, pl.ds(c, 512)] = a
        return acc + lane_fold(a)

    acc = lax.fori_loop(0, CL // 512, a2_step, jnp.zeros((S, 128), F32))
    m.dsrc[...] = to_row(jnp.sum(acc, 1, keepdims=True), S)
    c_den = start([(m.dsrc, m.drecv.at[d], dev) for d, dev in enumerate(pdev)])
    arrive(c_tea)

    for k in range(PAIRS):
        rows = jnp.broadcast_to(m.meta[z], (4, RPR, 128)).reshape(4 * RPR, 128)
        mine = iota((4, RPR, 128), 2) == iota((4, RPR, 128), 1) + k * RPR
        col = jnp.sum(jnp.where(mine.reshape(4 * RPR, 128), rows, 0.0), 1, keepdims=True)
        hot = jnp.where(iota((4 * RPR, 128), 1).astype(F32) == col, 1.0, 0.0).astype(BF)
        got = dot(hot, m.tq[2 * k:2 * k + 2].reshape(2 * T, D)).astype(BF)
        m.tss[:, k * RPR:(k + 1) * RPR, :] = got.reshape(4, RPR, D)
    m.ts[qd] = m.tss[qd]
    c_ts = start([(m.tss.at[q], m.ts.at[qd], dev) for q, dev in zip(qs, qdev)])

    u1 = row_factor(0, c_rs)
    uc1 = to_col(u1, 4 * T)
    for c in range(0, CQ, 256):
        m.cs[1, :, c:c + 256] = jnp.sum(m.e8[:, c:c + 256] * uc1, 0, keepdims=True)
    c_cs = start([(m.cs.at[1], m.csr.at[1, d], dev) for d, dev in enumerate(zdev)])

    arrive(c_den)
    den = m.dsrc[...]
    for d in range(NP - 1):
        den = den + m.drecv[d]
    sc2 = GS / to_col(den, S)
    scs = jnp.sum(m.pt[...] * sc2, 0, keepdims=True)
    for q in range(4):
        m.dq[q] = jnp.concatenate([scs[:, q * 64:(q + 1) * 64], spare], 1)
    m.dm[z, qd] = m.dq[qd]
    c_dq = start([(m.dq.at[q], m.dm.at[z, qd], dev) for q, dev in zip(qs, qdev)])

    next_ring()
    arrive(c_ts)
    m.tsh[...] = dot(m.pt[...].astype(BF), m.ts[...].reshape(S, D)).astype(BF)

    def t2_range(lo, hi):
        @pl.loop(lo, hi)
        def _(i):
            c = pl.multiple_of(i * 512, 512)
            m.t2[:, pl.ds(c, 512)] = jnp.exp(dot(m.tsh[...], m.w_b[:, pl.ds(c, 512)]) * (1.0 / teacher_temp))

    t2_range(0, CL // 512)
    arrive(c_dq)
    c_dz = start([(m.dm.at[z], m.dm.at[z], dev) for dev in zdev])

    v2 = col_factor(1, c_cs)
    m.va[qd] = v2
    c_rs = send_rowsum(1)
    c_va = start([(m.va.at[qd], m.va.at[qd], dev) for dev in qdev])
    while steps:
        next_ring()

    @pl.loop(0, PAIRS)
    def _(k):
        tk = m.tq[pl.ds(k * 2, 2)].reshape(2 * T, D)
        for c in range(0, CZ, 512):
            e = jnp.exp(dot(tk, m.wz[:, c:c + 512]) * (1.0 / teacher_temp))
            hi = e.astype(BF)
            m.esp[k, 0:128, c:c + 512] = hi
            m.esp[k, 128:256, c:c + 512] = (e - hi.astype(F32)).astype(BF)

    def block_col(ref, k):
        rows = jnp.broadcast_to(ref[...].reshape(NR, 1, 128), (NR, RPR, 128)).reshape(512, 128)
        mine = (iota((NR, RPR, 128), 2) == iota((NR, RPR, 128), 1) + k * RPR).reshape(512, 128)
        return jnp.sum(jnp.where(mine, rows, 0.0), 1, keepdims=True)

    vbase = pl.multiple_of(lax.rem(z, Z // 4) * CZ, CZ) if Z >= 4 else None

    def v_layout1(c):
        if Z >= 4:
            return m.va[z // (Z // 4), :, pl.ds(pl.multiple_of(vbase + c, 256), 256)]
        per = 4 // Z
        q = z * per + c // CQ
        return m.va[q, :, pl.ds(pl.multiple_of(c % CQ, 256), 256)]

    def layout1(k):
        sk = m.stu[:, :, pl.ds(pl.multiple_of(k * RPR, RPR), RPR), :].reshape(512, D)
        m.st[k] = sk.T
        ic = block_col(m.meta, k)
        m.idxc[k] = jnp.broadcast_to(ic, (512, 128))
        sc = block_col(m.dm, k)
        hot = jnp.where(iota((512, 128), 1).astype(F32) == ic, 1.0, 0.0).astype(BF)
        hot = jnp.concatenate([hot, hot], 1)

        @pl.loop(0, CZ // 256)
        def _(i):
            c = pl.multiple_of(i * 256, 256)
            m.a1[k, :, pl.ds(c, 256)] = jnp.exp(dot(sk, m.wz[:, pl.ds(c, 256)]) * (1.0 / student_temp)) * sc
            m.t1[k, :, pl.ds(c, 256)] = dot(hot, m.esp[k, :, pl.ds(c, 256)]) * v_layout1(c)

    u2 = row_factor(1, c_rs)
    m.ua[z] = u2 * (GS * TEACHERS)
    c_ua = start([(m.ua.at[z], m.ua.at[z], dev) for dev in zdev])
    arrive(c_va)
    arrive(c_metaz)
    arrive(c_dz)
    arrive(ring[-1])
    for k in range(PAIRS):
        layout1(k)
    arrive(c_ua)

    def quarter(z_, q):
        return m.ua[z_, :, q * T:(q + 1) * T]

    def own(z_):
        total = None
        for q in range(4):
            one = jnp.where(qd == q, quarter(z_, q), 0.0)
            total = one if total is None else total + one
        return total

    lane = iota((512, 128), 1).astype(F32)
    ucs = []
    for k in range(PAIRS):
        urow = jnp.concatenate([own(2 * k), own(2 * k + 1)], 1)
        ucs.append(jnp.sum(jnp.where(lane == m.idxc[k], jnp.broadcast_to(urow, (512, 128)), 0.0), 1, keepdims=True))

    def grad1(h):
        for c in range(h * CH, (h + 1) * CH, 256):
            total = None
            for k in range(PAIRS):
                g = (m.a1[k, :, c:c + 256] - m.t1[k, :, c:c + 256] * ucs[k]).astype(BF)
                one = dot(m.st[k], g)
                total = one if total is None else total + one
            at = c - h * CH
            m.ins[h, :, at:at + 256] = jnp.sum(m.wzf[:, c:c + 256] * total, 0, keepdims=True)
            for y_ in range(2):
                for z_ in range(Z):
                    for c_ in range(2):
                        f = ((y_ * Z + z_) * 2 + c_) * FB
                        m.gw[h, c_, y_, z_, :, at:at + 256] = total[f:f + FB, :]
        return (start([(m.gw.at[h, 1 - core], m.gwr.at[h], qdev[0])]),
                start([(m.ins.at[h], m.inr.at[h, d], dev) for d, dev in enumerate(qdev)]))

    c_gw, c_in, c_gy, c_gp = [None] * 2, [None] * 2, [None] * 2, [None] * 2
    c_gw[0], c_in[0] = grad1(0)
    c_gw[1], c_in[1] = grad1(1)

    def to_y(h):
        arrive(c_gw[h])
        m.gy[h] = m.gw[h, core, 1 - yl] + m.gwr[h, 1 - yl]
        c_gy[h] = start([(m.gy.at[h], m.gyr.at[h], qdev[1])])

    to_y(0)
    usort = []
    for q in range(4):
        for z_ in range(Z):
            usort.append(jnp.broadcast_to(quarter(z_, q), (B, T)))
    usort = jnp.concatenate(usort, 0)
    prow = m.msort[0][:, 0:64]
    for q in range(1, 4):
        prow = jnp.concatenate([prow, m.msort[q][:, 0:64]], 1)
    ztrow = jnp.broadcast_to(((iota((1, S), 1) >> (B.bit_length() - 1)) & 1).astype(F32) * T, (1, S))
    pcol = to_col(prow - ztrow, S)
    ucol = jnp.sum(jnp.where(iota((S, T), 1).astype(F32) == pcol, usort, 0.0), 1, keepdims=True)
    ucol = jnp.sum(m.pt[...] * to_row(ucol, S), 1, keepdims=True)

    def g2_step(i, acc):
        c = pl.multiple_of(i * 512, 512)
        q = (i * 512) // CQ
        w = min(512, CQ)
        if CQ >= 512:
            vv = m.va[q, :, pl.ds(pl.multiple_of(c - q * CQ, 512), 512)]
        else:
            vv = jnp.concatenate([m.va[q + j] for j in range(512 // CQ)], 1)
        g = (m.a2[:, pl.ds(c, 512)] * sc2 - m.t2[:, pl.ds(c, 512)] * vv * ucol).astype(BF)
        return acc + dotg(g, m.w_b[:, pl.ds(c, 512)], NT)

    gsum = lax.fori_loop(0, CL // 1024, g2_step, jnp.zeros((S, D), F32))
    to_y(1)
    gsum = lax.fori_loop(CL // 1024, CL // 512, g2_step, gsum)
    m.gu[...] = gsum.reshape(NP, RB, D)
    c_gu = start([(m.gu.at[p2], m.gur.at[d], dev) for d, (p2, dev) in enumerate(zip(ps, pdev))])

    def to_z(h):
        arrive(c_in[h])
        inner = m.ins[h] + m.inr[h, 0] + m.inr[h, 1] + m.inr[h, 2]
        arrive(c_gy[h])
        inv = 1.0 / m.nz[:, h * CH:(h + 1) * CH]
        for z_ in range(Z):
            f = pl.multiple_of(row(yl, z_, core) * FB, FB)
            mine = m.gw[h, core, yl, z_] + m.gwr[h, yl, z_] + m.gyr[h, z_]
            m.go[h, z_] = (mine - m.wzf[pl.ds(f, FB), h * CH:(h + 1) * CH] * inner) * inv
        m.gpr[h, z] = m.go[h, z]
        c_gp[h] = start([(m.go.at[h, z2], m.gpr.at[h, z], dev) for z2, dev in zip(zs, zdev)])

    to_z(0)

    arrive(c_gu)
    gsum = m.gu[p]
    for d in range(NP - 1):
        gsum = gsum + m.gur[d]
    su = stu_ref[pl.ds(pl.multiple_of(p * RB, RB), RB), :].astype(F32)
    un = jnp.sqrt(jnp.sum(su * su, 1, keepdims=True) + epsilon)
    su = su / un
    m.gsr[p] = (gsum - su * jnp.sum(su * gsum, 1, keepdims=True)) / un
    c_gs = start([(m.gsr.at[p], m.gsr.at[p], dev) for dev in pdev])

    to_z(1)
    for h in range(2):
        arrive(c_gp[h])
        for z_ in range(Z):
            c = z_ * CZ + h * CH
            gp_out[:, c:c + CH] = m.gpr[h, z_]
    arrive(c_gs)
    gs_out[...] = m.gsr[...].reshape(S, D)
    for h in sent:
        h.wait_send()


def body(teacher, students, prototypes, pairing, layout):
    NR = lax.axis_size("rows")
    NP = lax.axis_size("protos")
    T, D = teacher.shape
    S = students.shape[0]
    CL = prototypes.shape[1]
    dims = (NR, NP, T, S, D, CL)
    vmem = pl.BlockSpec(memory_space=pltpu.VMEM)
    scratch = [pltpu.VMEM(shape, dtype) for shape, dtype in plan(*dims).values()]
    scratch += [pltpu.SemaphoreType.DMA((NSEM,)), pltpu.SemaphoreType.DMA((NSEM,)), pltpu.SemaphoreType.DMA((5,))]
    return pl.pallas_call(
        functools.partial(kernel, dims),
        out_shape=(
            jax.ShapeDtypeStruct((S, D), F32),
            jax.ShapeDtypeStruct((D // NR, CL), F32),
        ),
        in_specs=[pl.BlockSpec(memory_space=pl.ANY)] * 5,
        out_specs=(vmem, vmem),
        scratch_shapes=scratch,
        compiler_params=pltpu.CompilerParams(
            collective_id=0, has_side_effects=True, vmem_limit_bytes=VMEM_MIB * 1024 * 1024
        ),
        name="distill",
    )(teacher, students, prototypes, layout.reshape(1, S), pairing.reshape(1, S))


def solution(mesh):
    in_specs = (P("rows", None), P("rows", None), P(None, "protos"), P("rows"), P("rows"))
    out_specs = (P("rows", None), P("rows", "protos"))
    return jax.shard_map(body, mesh=mesh, in_specs=in_specs, out_specs=out_specs, check_vma=False)
```
